256 devices in a mesh: grp: 64 (over y, x, z_lo, core), con: 4 (over z_hi).
Axes of the slice: x: 4, y: 4, z: 8 (z_hi: 4, z_lo: 2; z = z_hi * 2 + z_lo), core: 2. Of those that a mesh axis runs over, the one named last changes fastest.
Arguments:
- amplitudes: bfloat16 [1600, 384, 384], P('grp', None, 'con'), may hold values from -6 to 6
- integrals: bfloat16 [40, 384, 3, 384], P(None, 'con'), may hold values from -0.046875 to 0.046875
- occ_energy: float32 [40], replicated, may hold values from -2 to -0.5
- vir_energy: float32 [384], replicated, may hold values from 0.2 to 3
- occ_irrep: int32 [40], replicated, may hold values from 0 to 7
- vir_irrep: int32 [384], replicated, may hold values from 0 to 7, as said below
Outputs:
- update: float32 [40, 3, 384, 384], P('con', None, 'grp')
The draws below stay inside these ranges and needn't reach their ends.
Inputs may be any that keep to these rules, and one draw needn't show every extreme that they name: `occ_irrep`: D2h labels as 3-bit numbers; the product of two irreducible representations is the exclusive or of their labels. `vir_irrep`: D2h labels as 3-bit numbers; at most 192 virtual orbitals share one label, and some label is shared by exactly that many.
All inputs are finite; a program needn't handle non-finite values.
Results may differ from the reference program's by a relative error of at most 0.0031.
Values may be sent and summed in bfloat16 or wider, within the bound.
No kernel may reach another device: no remote copies, remote signals or barrier semaphores. Data moves between devices by JAX's collectives and lax.ppermute only.
A program may use at most 128 MiB of HBM per device.

```python
import jax
import jax.numpy as jnp
from jax import lax

OCC = 40
VIR = 384
OJW = 3
PAIRS = 1600


def draw_vir_irrep(key, part):
    crowd_key = jax.random.fold_in(key, 11)
    other_key = jax.random.fold_in(key, 12)
    place_key = jax.random.fold_in(key, 13)
    crowded_label = jax.random.randint(crowd_key, (), 0, 8, dtype=jnp.int32)
    others = jnp.bitwise_xor(crowded_label, jax.random.randint(other_key, (VIR,), 1, 8, dtype=jnp.int32))
    position = jnp.arange(VIR, dtype=jnp.int32)
    by_position = jnp.where(position < VIR // 2, crowded_label, others)
    shuffle = jax.random.permutation(place_key, VIR)
    return by_position[shuffle].astype(jnp.int32)


def touch_ends(array, rng, low, top_value):
    dims = array.shape
    index_at = [jax.random.randint(jax.random.fold_in(rng, axis), (), 0, dims[axis]) for axis in range(len(dims))]
    array = array.at[tuple(index_at)].set(low)
    longest = dims.index(max(dims))
    index_at[longest] = (index_at[longest] + 1) % dims[longest]
    return array.at[tuple(index_at)].set(top_value)


def block_levels(key, dims, cuts, smallest, largest):
    gain, own = 1.0, jax.random.fold_in(key, 6)
    for dim, blocks in cuts:
        heights = jnp.exp(jax.random.uniform(jax.random.fold_in(own, dim), (blocks,), jnp.float32, smallest / len(cuts), largest / len(cuts)))
        gain = gain * jnp.repeat(heights, dims[dim] // blocks).reshape([-1 if axis == dim else 1 for axis in range(len(dims))])
    return gain


def normal_values(stream_key, dims, spread, most, shards=(), kind=jnp.bfloat16):
    values = jax.random.normal(stream_key, dims, jnp.float32) * spread
    if len(shards) > 0:
        values = block_levels(stream_key, dims, shards, -0.22, 0.18) * values
    return jnp.clip(values, min=-most, max=most).astype(kind)


def setup_inputs(seed: int = 0) -> dict:
    streams_of = jax.random.split(jax.random.key(seed), 7)
    amplitudes = normal_values(streams_of[0], (PAIRS, VIR, VIR), 1.0, 6.0, ((0, 64), (2, 4)))
    integrals = normal_values(streams_of[1], (OCC, VIR, OJW, VIR), (OCC * VIR) ** -0.5, 0.046875, ((1, 4),))
    occ_energy = jnp.clip(jax.random.uniform(streams_of[2], (OCC,), jnp.float32, -2.0, -0.5), -2.0, -0.5)
    vir_energy = jnp.clip(jax.random.uniform(streams_of[3], (VIR,), jnp.float32, 0.2, 3.0), 0.2, 3.0)
    occ_irrep = touch_ends(jax.random.randint(streams_of[4], (OCC,), 0, 8), jax.random.fold_in(streams_of[4], 1), 0, 7).astype(jnp.int32)
    vir_irrep = draw_vir_irrep(jax.random.fold_in(streams_of[6], 71), 0)
    return {"amplitudes": amplitudes, "integrals": integrals, "occ_energy": occ_energy, "vir_energy": vir_energy, "occ_irrep": occ_irrep, "vir_irrep": vir_irrep}


def reference(amplitudes, integrals, occ_energy, vir_energy, occ_irrep, vir_irrep):
    pair_block = amplitudes.reshape(OCC, OCC, VIR, VIR)
    weights = integrals.astype(jnp.float32)

    def one_occupied(occ_index):
        direct = pair_block[occ_index].astype(jnp.float32)
        crossed = pair_block[:, occ_index].astype(jnp.float32)
        combined = (2.0 * direct - crossed).astype(jnp.bfloat16)
        combined = lax.optimization_barrier(combined).astype(jnp.float32)
        return jnp.einsum("kac,kcjb->jab", combined, weights)

    cycle_term = lax.map(one_occupied, jnp.arange(OCC, dtype=jnp.int32))
    occ_window = occ_energy[:OJW]
    denominator = (occ_energy[:, None, None, None] + occ_window[None, :, None, None]
                   - vir_energy[None, None, :, None] - vir_energy[None, None, None, :])
    label = jnp.bitwise_xor(occ_irrep[:, None, None, None], occ_irrep[:OJW][None, :, None, None])
    label = jnp.bitwise_xor(label, vir_irrep[None, None, :, None])
    label = jnp.bitwise_xor(label, vir_irrep[None, None, None, :])
    symmetric = (label == 0).astype(jnp.float32)
    return symmetric * cycle_term / denominator
```

```python
import functools

import jax
import jax.numpy as jnp
from jax import lax
from jax.experimental import pallas as pl
from jax.experimental.pallas import tpu as pltpu
from jax.sharding import PartitionSpec as P

OCC = 40
VIR = 384
OJW = 3
GRP = 64
CON = 4
PAIR = OCC * OCC // GRP
SEC = VIR // GRP
CW = VIR // CON
OWN = OCC // CON
SLOT = VIR // 2
TILES = 19
MSG = 120
VMEM = pl.BlockSpec(memory_space=pltpu.VMEM)
SMEM = pl.BlockSpec(memory_space=pltpu.SMEM)
HBM = pl.BlockSpec(memory_space=pl.ANY)
LIMIT = 56 * 1024 * 1024


def nt_dot(x, y):
    return lax.dot_general(x, y, (((1,), (1,)), ((), ())), preferred_element_type=jnp.float32)


def pack_kernel(x_ref, out_ref, main_ref, rest_ref):
    for t in range(TILES):
        group, j = divmod(t, 4)
        quad, q = divmod(t, 3)
        if j < 3:
            dst, at = main_ref.at[j], group * 128
        else:
            dst, at = rest_ref, group * 128
        dst[at : at + 96, :] = x_ref[4 * quad + q]
        if 4 * quad + 3 < PAIR:
            dst[at + 96 : at + 128, :] = x_ref[4 * quad + 3, 32 * q : 32 * q + 32, :]
        else:
            dst[at + 96 : at + 128, :] = jnp.zeros((32, VIR), jnp.bfloat16)
    row = lax.broadcasted_iota(jnp.int32, (GRP * 8, VIR), 0)
    col = lax.broadcasted_iota(jnp.int32, (GRP * 8, VIR), 1)
    dest, sub = row // 8, row % 8
    pick = jnp.where((sub < 6) & (col == dest * 6 + sub), 1.0, 0.0).astype(jnp.bfloat16)
    for j in range(3):
        pick_rest = jnp.where((sub >= 6) & (col == dest * 6 + 2 * j + sub - 6), 1.0, 0.0).astype(jnp.bfloat16)
        main = nt_dot(pick, main_ref[j])
        rest = nt_dot(pick_rest, rest_ref[...])
        for group in range(5):
            tile = main[:, group * 128 : group * 128 + 128]
            if group < 4:
                tile = tile + rest[:, group * 128 : group * 128 + 128]
            at = (group * 3 + j) * 8
            out_ref[:, at : at + 8, :] = tile.astype(jnp.bfloat16).reshape(GRP, 8, 128)


def pack(x):
    return pl.pallas_call(
        pack_kernel,
        out_shape=jax.ShapeDtypeStruct((GRP, MSG, 128), jnp.bfloat16),
        in_specs=[VMEM],
        out_specs=VMEM,
        scratch_shapes=[
            pltpu.VMEM((3, 640, VIR), jnp.bfloat16),
            pltpu.VMEM((512, VIR), jnp.bfloat16),
        ],
        compiler_params=pltpu.CompilerParams(vmem_limit_bytes=LIMIT),
        name="pack",
    )(x)


def own_column(ref, first, dtype):
    row = lax.broadcasted_iota(jnp.int32, (8, 1), 0)
    column = jnp.zeros((8, 1), dtype)
    for a in range(SEC):
        column = jnp.where(row == a, ref[first + a], column)
    return column


def term_kernel(where_ref, occ_ref, vir_ref, label_ref, got_ref, w_hbm, *refs):
    outs, fold_ref, (pairs_ref, w_ref, lhs_ref, sum_ref, sems) = refs[:5], refs[5], refs[6:]
    me = where_ref[1]

    def fetch(kq, carry):
        for q in range(3):
            for j in range(OJW):
                at = pl.multiple_of(kq % 2 * 384, 384) + q * 128
                lanes = pl.ds(j * VIR, VIR)
                pltpu.make_async_copy(
                    w_hbm.at[4 * kq + q, j], w_ref.at[kq // 2, pl.ds(at, 96), lanes], sems.at[kq // 2]
                ).start()
                pltpu.make_async_copy(
                    w_hbm.at[4 * kq + 3, j, pl.ds(32 * q, 32)],
                    w_ref.at[kq // 2, pl.ds(at + 96, 32), lanes],
                    sems.at[kq // 2],
                ).start()
        return carry

    lax.fori_loop(0, 10, fetch, 0)

    sub = lax.broadcasted_iota(jnp.int32, (8, 128), 0)
    lane = lax.broadcasted_iota(jnp.int32, (8, 128), 1)

    def unpack(s, carry):
        got = got_ref[s].astype(jnp.float32).reshape(15, 8, 128)
        tiles = []
        for t in range(TILES):
            group, j = divmod(t, 4)
            if j < 3:
                tiles.append(got[3 * group + j])
            else:
                a, b, c = (pltpu.roll(got[3 * group + n], 2 + 2 * n, 0) for n in range(3))
                tiles.append(jnp.where(sub < 2, a, jnp.where(sub < 4, b, c)))
        for p in range(PAIR):
            quad, q = divmod(p, 4)
            if q < 3:
                value = tiles[3 * quad + q]
            else:
                a, b, c = (pltpu.roll(tiles[3 * quad + n], 32 + 32 * n, 1) for n in range(3))
                value = jnp.where(lane < 32, a, jnp.where(lane < 64, b, c))
            pairs_ref[PAIR * s + p] = value
        return carry

    lax.fori_loop(0, GRP, unpack, 0)

    lane3 = lax.broadcasted_iota(jnp.int32, (OCC, 8, 128), 2)
    by_i = pairs_ref.reshape(OCC, OCC, 8, 128)

    def combine(kq, carry):
        combined = []
        for q in range(4):
            k = 4 * kq + q
            direct, crossed = by_i[:, k], by_i[k]
            combined.append(2.0 * direct - crossed)
        for q in range(3):
            rolled = pltpu.roll(combined[3], 96 - 32 * q, 2)
            merged = jnp.where(lane3 < 96, combined[q], rolled)
            at = pl.multiple_of(kq % 2 * 384, 384) + q * 128
            lhs_ref[kq // 2, :, pl.ds(at, 128)] = merged.reshape(OCC * 8, 128).astype(jnp.bfloat16)
        return carry

    lax.fori_loop(0, 10, combine, 0)

    def multiply(b, carry):
        pltpu.make_async_copy(w_ref.at[b], w_ref.at[b], sems.at[b]).wait()
        part = jnp.dot(lhs_ref[b], w_ref[b], preferred_element_type=jnp.float32)

        @pl.when(b == 0)
        def _():
            sum_ref[...] = part

        @pl.when(b > 0)
        def _():
            sum_ref[...] += part

        return carry

    lax.fori_loop(0, 5, multiply, 0)

    labels = label_ref[...]
    label_row = labels.astype(jnp.float32)
    label_col = jnp.transpose(jnp.broadcast_to(label_row, (8, VIR)))[:, :1]
    first = lax.broadcasted_iota(jnp.int32, (VIR, VIR), 0)
    second = lax.broadcasted_iota(jnp.int32, (VIR, VIR), 1)
    ahead = (label_col < label_row) | ((label_col == label_row) & (first < second))
    rank = jnp.sum(jnp.where(ahead, 1.0, 0.0), axis=0, keepdims=True)
    slot = jnp.where(rank >= SLOT, rank - SLOT, rank).astype(jnp.int32)
    fold = jnp.where(lax.broadcasted_iota(jnp.int32, (SLOT, VIR), 0) == slot, 1.0, 0.0).astype(jnp.bfloat16)
    fold_ref[...] = fold

    label_ab = own_column(vir_ref, where_ref[0] * SEC, jnp.int32) ^ labels

    def mask(i, carry):
        rows = pl.ds(pl.multiple_of(i * 8, 8), 8)
        for j in range(OJW):
            lanes = pl.ds(j * VIR, VIR)
            keep = label_ab == (occ_ref[i] ^ occ_ref[j])
            sum_ref[rows, lanes] = jnp.where(keep, sum_ref[rows, lanes], 0.0)
        return carry

    lax.fori_loop(0, OCC, mask, 0)

    row = lax.broadcasted_iota(jnp.int32, (64, OWN * 8), 0)
    col = lax.broadcasted_iota(jnp.int32, (64, OWN * 8), 1)
    dense = jnp.where((row < OWN * SEC) & (col == row // SEC * 8 + row % SEC), 1.0, 0.0).astype(jnp.bfloat16)
    for s in range(CON):
        owner = lax.rem(me + s, CON)
        rows = pl.ds(pl.multiple_of(owner * (OWN * 8), 8), OWN * 8)
        for j in range(OJW):
            value = sum_ref[rows, j * VIR : (j + 1) * VIR]
            high = value.astype(jnp.bfloat16)
            parts = [(outs[s], high)]
            if s == 0:
                parts.append((outs[4], (value - high.astype(jnp.float32)).astype(jnp.bfloat16)))
            for out, part in parts:
                part = jnp.dot(dense, part, preferred_element_type=jnp.float32).astype(jnp.bfloat16)
                out[:, j * SLOT : (j + 1) * SLOT] = nt_dot(part, fold).astype(jnp.bfloat16)


def term(where, occ_irrep, vir_irrep, label_row, got, w):
    chunk = jax.ShapeDtypeStruct((64, OJW * SLOT), jnp.bfloat16)
    return pl.pallas_call(
        term_kernel,
        out_shape=[chunk] * 5 + [jax.ShapeDtypeStruct((SLOT, VIR), jnp.bfloat16)],
        in_specs=[SMEM, SMEM, SMEM, VMEM, VMEM, HBM],
        out_specs=[VMEM] * 6,
        scratch_shapes=[
            pltpu.VMEM((OCC * OCC, 8, 128), jnp.float32),
            pltpu.VMEM((5, 768, OJW * VIR), jnp.bfloat16),
            pltpu.VMEM((5, OCC * 8, 768), jnp.bfloat16),
            pltpu.VMEM((OCC * 8, OJW * VIR), jnp.float32),
            pltpu.SemaphoreType.DMA((5,)),
        ],
        compiler_params=pltpu.CompilerParams(vmem_limit_bytes=LIMIT),
        name="term",
    )(where, occ_irrep, vir_irrep, label_row, got, w)


def finish_kernel(where_ref, occ_ref, vir_ref, occ_e_ref, vir_e_ref, label_ref, energy_ref, fold_ref, *refs):
    chunks, out_ref = refs[:5], refs[5]
    first = where_ref[1] * OWN
    label_ab = (own_column(vir_ref, where_ref[0] * SEC, jnp.int32) ^ label_ref[...])[:SEC]
    energy_a = own_column(vir_e_ref, where_ref[0] * SEC, jnp.float32)[:SEC]
    for j in range(OJW):
        total = jnp.zeros((64, VIR), jnp.float32)
        for chunk in chunks:
            total += jnp.dot(
                chunk[:, j * SLOT : (j + 1) * SLOT], fold_ref[...], preferred_element_type=jnp.float32
            )
        for i in range(OWN):
            keep = label_ab == (occ_ref[first + i] ^ occ_ref[j])
            denominator = occ_e_ref[first + i] + occ_e_ref[j] - energy_a - energy_ref[...]
            out_ref[i, j] = jnp.where(keep, total[i * SEC : (i + 1) * SEC], 0.0) / denominator


def finish(where, occ_irrep, vir_irrep, occ_energy, vir_energy, label_row, energy_row, fold, chunks):
    return pl.pallas_call(
        finish_kernel,
        out_shape=jax.ShapeDtypeStruct((OWN, OJW, SEC, VIR), jnp.float32),
        in_specs=[SMEM] * 5 + [VMEM] * 8,
        out_specs=VMEM,
        compiler_params=pltpu.CompilerParams(vmem_limit_bytes=LIMIT),
        name="finish",
    )(where, occ_irrep, vir_irrep, occ_energy, vir_energy, label_row, energy_row, fold, *chunks)


def shards(amplitudes, integrals, occ_energy, vir_energy, occ_irrep, vir_irrep):
    where = jnp.stack([lax.axis_index("grp"), lax.axis_index("con")]).astype(jnp.int32)
    label_row, energy_row = vir_irrep.reshape(1, VIR), vir_energy.reshape(1, VIR)
    sent = pack(jnp.swapaxes(amplitudes, 1, 2))
    got = lax.all_to_all(sent, "grp", split_axis=0, concat_axis=0, tiled=True)
    *chunks, fold = term(where, occ_irrep, vir_irrep, label_row, got, jnp.swapaxes(integrals, 1, 2))
    arrived = [chunks[0], chunks[4]]
    for s in range(1, CON):
        arrived.append(lax.ppermute(chunks[s], "con", [(n, (n + s) % CON) for n in range(CON)]))
    return finish(where, occ_irrep, vir_irrep, occ_energy, vir_energy, label_row, energy_row, fold, arrived)


def solution(mesh):
    return jax.shard_map(
        shards,
        mesh=mesh,
        in_specs=(P("grp", None, "con"), P(None, "con", None, None), P(), P(), P(), P()),
        out_specs=P("con", None, "grp", None),
        check_vma=False,
    )
```

```python
import jax
import jax.numpy as jnp
from jax import lax
from jax.experimental import pallas as pl
from jax.experimental.pallas import tpu as pltpu
from jax.sharding import PartitionSpec as P


OCC = 40
VIR = 384
OJW = 3
GRP = 64
CON = 4
PAIR = OCC * OCC // GRP
SEC = VIR // GRP
OWN = OCC // CON
SLOT = VIR // 2
WIDE = OJW * VIR
VMEM = pl.BlockSpec(memory_space=pltpu.VMEM)
SMEM = pl.BlockSpec(memory_space=pltpu.SMEM)
HBM = pl.BlockSpec(memory_space=pltpu.HBM)
MIB = 1024 * 1024
BF16, F32 = jnp.bfloat16, jnp.float32

COUPLES = 13
A_WIDTH, A_ROWS, A_BLOCK, A_STEPS = 64, 80, 512, 5
B_WIDTH, B_ROWS, B_BLOCK, B_STEPS = 32, 48, 640, 2


def nt_dot(x, y):
    return lax.dot_general(x, y, (((1,), (1,)), ((), ())), preferred_element_type=F32)


def picks():
    row = lax.broadcasted_iota(jnp.int32, (GRP * 8, 1), 0)
    dest, sub = row // 8, row % 8
    col = lax.broadcasted_iota(jnp.int32, (GRP * 8, VIR), 1)

    def pick(target):
        return jnp.where(col == target, 1.0, 0.0).astype(BF16)

    main = pick(jnp.where(sub < 6, dest * SEC + sub, -1))
    return main, [pick(jnp.where(sub >= 6, dest * SEC + 2 * j + sub - 6, -1)) for j in range(3)]


def store_tiles(out_ref, value, tile):
    out_ref[:, tile * 8 : tile * 8 + 8, :] = value.astype(BF16).reshape(GRP, 8, 128)


def pack_kernel(tiles, with_rest, pieces, first_c, width, x_hbm, out_ref, main_ref, rest_ref, sem):
    odd = lax.rem(lax.axis_index("grp"), 2)

    def fetch(lane_tile, dst, at):
        for n in range(pieces):
            pair = jnp.clip(pieces * lane_tile + n - odd, 0, PAIR - 1)
            pltpu.make_async_copy(
                x_hbm.at[pair, pl.ds(first_c, width)], dst.at[pl.ds(at + n * width, width)], sem
            ).start()

    for j in range(3):
        for n, lane_tile in enumerate(tiles[j]):
            fetch(lane_tile, main_ref.at[j], n * 128)
    for n, lane_tile in enumerate(with_rest):
        fetch(lane_tile, rest_ref, n * 128)
    main_pick, rest_picks = picks()
    for j in range(3):
        size = len(tiles[j]) * 128
        whole = main_ref.at[j, pl.ds(0, size)]
        pltpu.make_async_copy(whole, whole, sem).wait()
    pltpu.make_async_copy(rest_ref, rest_ref, sem).wait()
    for j in range(3):
        main = nt_dot(main_pick, main_ref[j, : len(tiles[j]) * 128])
        rest = nt_dot(rest_picks[j], rest_ref[...])
        for n in range(len(tiles[j])):
            value = main[:, n * 128 : n * 128 + 128]
            if n < len(with_rest):
                value = value + rest[:, n * 128 : n * 128 + 128]
            store_tiles(out_ref, value, 3 * n + j)


A_TILES, A_REST = ((0, 4, 8, 12), (1, 5, 9), (2, 6, 10)), (3, 7, 11)
B_TILES, B_REST = ((0, 4), (1, 5), (2, 6)), (3,)


def pack(x, rows, tiles, rest, pieces, first_c, width):
    def kernel(*refs):
        pack_kernel(tiles, rest, pieces, first_c, width, *refs)

    return pl.pallas_call(
        kernel,
        out_shape=jax.ShapeDtypeStruct((GRP, rows, 128), BF16),
        in_specs=[HBM],
        out_specs=VMEM,
        scratch_shapes=[
            pltpu.VMEM((3, len(tiles[0]) * 128, VIR), BF16),
            pltpu.VMEM((len(rest) * 128, VIR), BF16),
            pltpu.SemaphoreType.DMA,
        ],
        compiler_params=pltpu.CompilerParams(vmem_limit_bytes=12 * MIB),
        cost_estimate=pl.CostEstimate(flops=10**9, bytes_accessed=3 * 10**6, transcendentals=0),
    )(x)


def own_column(ref, first, dtype):
    row = lax.broadcasted_iota(jnp.int32, (8, 1), 0)
    column = jnp.zeros((8, 1), dtype)
    for a in range(SEC):
        column = jnp.where(row == a, ref[first + a], column)
    return column


def prepare_kernel(
    occ_ref, vir_ref, occ_e_ref, vir_e_ref, label_ref, energy_ref, w_hbm, wa_ref, wb_ref, fold_ref, scale_ref, sem
):
    def fetch(kq, carry):
        for n in range(4):
            for j in range(OJW):
                source = w_hbm.at[4 * kq + n, j]
                lanes = pl.ds(j * VIR, VIR)
                at_a = pl.multiple_of(kq * 256 + n * A_WIDTH, A_WIDTH)
                at_b = pl.multiple_of(kq * 128 + n * B_WIDTH, B_WIDTH)
                pltpu.make_async_copy(
                    source.at[pl.ds(0, A_WIDTH)], wa_ref.at[pl.ds(at_a, A_WIDTH), lanes], sem.at[0]
                ).start()
                pltpu.make_async_copy(
                    source.at[pl.ds(A_WIDTH, B_WIDTH)], wb_ref.at[pl.ds(at_b, B_WIDTH), lanes], sem.at[1]
                ).start()
        return carry

    lax.fori_loop(0, 10, fetch, 0)

    labels = label_ref[...]
    label_row = labels.astype(F32)
    label_col = jnp.transpose(jnp.broadcast_to(label_row, (8, VIR)))[:, :1]
    first = lax.broadcasted_iota(jnp.int32, (VIR, VIR), 0)
    second = lax.broadcasted_iota(jnp.int32, (VIR, VIR), 1)
    ahead = (label_col < label_row) | ((label_col == label_row) & (first < second))
    rank = jnp.sum(jnp.where(ahead, 1.0, 0.0), axis=0, keepdims=True)
    slot = jnp.where(rank >= SLOT, rank - SLOT, rank).astype(jnp.int32)
    fold_ref[...] = jnp.where(lax.broadcasted_iota(jnp.int32, (SLOT, VIR), 0) == slot, 1.0, 0.0).astype(BF16)

    own_i, own_a = lax.axis_index("con") * OWN, lax.axis_index("grp") * SEC
    label_ab = (own_column(vir_ref, own_a, jnp.int32) ^ labels)[:SEC]
    energy_ab = (own_column(vir_e_ref, own_a, F32) + energy_ref[...])[:SEC]
    for i in range(OWN):
        for j in range(OJW):
            keep = label_ab == (occ_ref[own_i + i] ^ occ_ref[j])
            denominator = occ_e_ref[own_i + i] + occ_e_ref[j] - energy_ab
            scale_ref[i, j] = jnp.where(keep, 1.0, 0.0) / denominator

    pltpu.make_async_copy(wa_ref, wa_ref, sem.at[0]).wait()
    pltpu.make_async_copy(wb_ref, wb_ref, sem.at[1]).wait()


def prepare(occ_irrep, vir_irrep, occ_energy, vir_energy, w):
    return pl.pallas_call(
        prepare_kernel,
        out_shape=[
            jax.ShapeDtypeStruct((OCC * A_WIDTH, WIDE), BF16),
            jax.ShapeDtypeStruct((OCC * B_WIDTH, WIDE), BF16),
            jax.ShapeDtypeStruct((SLOT, VIR), BF16),
            jax.ShapeDtypeStruct((OWN, OJW, SEC, VIR), F32),
        ],
        in_specs=[SMEM] * 4 + [VMEM] * 2 + [HBM],
        out_specs=[VMEM] * 4,
        scratch_shapes=[pltpu.SemaphoreType.DMA((2,))],
        compiler_params=pltpu.CompilerParams(vmem_limit_bytes=24 * MIB),
        cost_estimate=pl.CostEstimate(flops=10**8, bytes_accessed=20 * 10**6, transcendentals=0),
        name="prepare",
    )(
        occ_irrep,
        vir_irrep,
        occ_energy,
        vir_energy,
        vir_irrep.reshape(1, VIR),
        vir_energy.reshape(1, VIR),
        w,
    )


def lane_tiles(got_ref, s, rows, tiles, with_rest):
    got = got_ref[s].astype(F32).reshape(rows // 8, 8, 128)
    sub = lax.broadcasted_iota(jnp.int32, (8, 128), 0)
    found = {}
    for j in range(3):
        for n, lane_tile in enumerate(tiles[j]):
            found[lane_tile] = got[3 * n + j]
    for n, lane_tile in enumerate(with_rest):
        a, b, c = (pltpu.roll(got[3 * n + j], 2 + 2 * j, 0) for j in range(3))
        found[lane_tile] = jnp.where(sub < 2, a, jnp.where(sub < 4, b, c))
    return [found[t] for t in range(len(found))]


def store_couples(h, even, odd, half, couple_ref):
    lane = lax.broadcasted_iota(jnp.int32, (8, 128), 1)
    for u in range(COUPLES - 1):
        couple_ref[PAIR * h + u] = even[u]
        couple_ref[PAIR * h + COUPLES + u] = odd[u + 1]
    couple_ref[PAIR * h + COUPLES - 1] = jnp.where(lane < half, even[COUPLES - 1], odd[0])


def store_rows(lhs_ref, step, at, even, odd):
    half = OCC // 2 * 8
    lhs_ref[step, :half, pl.ds(at, 128)] = even.reshape(half, 128).astype(BF16)
    lhs_ref[step, half:, pl.ds(at, 128)] = odd.reshape(half, 128).astype(BF16)


def term_a_kernel(got_ref, w_ref, sum_ref, couple_ref, lhs_ref):
    def unpack(h, carry):
        even, odd = (lane_tiles(got_ref, 2 * h + n, A_ROWS, A_TILES, A_REST) for n in range(2))
        store_couples(h, even, odd, 64, couple_ref)
        return carry

    lax.fori_loop(0, GRP // 2, unpack, 0)

    lane = lax.broadcasted_iota(jnp.int32, (OCC // 2, 8, 128), 2)
    by_i = couple_ref.reshape(OCC, OCC // 2, 8, 128)
    by_parity = couple_ref.reshape(OCC // 2, 2, OCC // 2, 8, 128)

    def combine(kk, carry):
        first, second = by_i[2 * kk], by_i[2 * kk + 1]
        even = jnp.where(lane < 64, first, pltpu.roll(second, 64, 2))
        odd = jnp.where(lane < 64, pltpu.roll(first, 64, 2), second)
        even = 2.0 * by_parity[:, 0, kk] - even
        odd = 2.0 * by_parity[:, 1, kk] - odd
        store_rows(lhs_ref, kk // 4, pl.multiple_of(kk % 4 * 128, 128), even, odd)
        return carry

    lax.fori_loop(0, OCC // 2, combine, 0)
    multiply(lhs_ref, w_ref, sum_ref, A_BLOCK, A_STEPS, None)


def multiply(lhs_ref, w_ref, sum_ref, block, steps, before_ref):
    def body(b, carry):
        rows = pl.ds(pl.multiple_of(b * block, block), block)
        part = jnp.dot(lhs_ref[b], w_ref[rows, :], preferred_element_type=F32)

        @pl.when(b == 0)
        def _():
            sum_ref[...] = part if before_ref is None else before_ref[...] + part

        @pl.when(b > 0)
        def _():
            sum_ref[...] += part

        return carry

    lax.fori_loop(0, steps, body, 0)


def term_a(got, w):
    return pl.pallas_call(
        term_a_kernel,
        out_shape=jax.ShapeDtypeStruct((OCC * 8, WIDE), F32),
        in_specs=[VMEM] * 2,
        out_specs=VMEM,
        scratch_shapes=[
            pltpu.VMEM((OCC * OCC // 2, 8, 128), F32),
            pltpu.VMEM((A_STEPS, OCC * 8, A_BLOCK), BF16),
        ],
        compiler_params=pltpu.CompilerParams(vmem_limit_bytes=14 * MIB),
        cost_estimate=pl.CostEstimate(flops=2 * 10**9, bytes_accessed=20 * 10**6, transcendentals=0),
        name="term_a",
    )(got, w)


def term_b_kernel(occ_ref, vir_ref, label_ref, got_ref, w_ref, fold_ref, before_ref, *refs):
    outs, (couple_ref, lhs_ref, sum_ref) = refs[:5], refs[5:]
    me = lax.axis_index("con")

    def unpack(h, carry):
        both = []
        for n in range(2):
            tiles = lane_tiles(got_ref, 2 * h + n, B_ROWS, B_TILES, B_REST)
            rolled = [pltpu.roll(t, 64, 1) for t in tiles]
            both.append([(tiles, rolled)[u % 2][u // 2] for u in range(COUPLES)])
        store_couples(h, *both, 32, couple_ref)
        return carry

    lax.fori_loop(0, GRP // 2, unpack, 0)

    lane = lax.broadcasted_iota(jnp.int32, (OCC // 2, 8, 128), 2)
    by_i = couple_ref.reshape(OCC, OCC // 2, 8, 128)
    by_parity = couple_ref.reshape(OCC // 2, 2, OCC // 2, 8, 128)

    def quarters(parts):
        low = jnp.where(lane < 32, parts[0], parts[1])
        high = jnp.where(lane < 96, parts[2], parts[3])
        return jnp.where(lane < 64, low, high)

    def combine(kq, carry):
        crossed = [by_i[4 * kq + n] for n in range(4)]
        values = []
        for parity in range(2):
            parts = [
                crossed[n] if n == parity else pltpu.roll(crossed[n], (32 * (n - parity)) % 128, 2) for n in range(4)
            ]
            direct = jnp.where(
                lane < 64, by_parity[:, parity, 2 * kq], pltpu.roll(by_parity[:, parity, 2 * kq + 1], 64, 2)
            )
            values.append(2.0 * direct - quarters(parts))
        store_rows(lhs_ref, kq // 5, pl.multiple_of(kq % 5 * 128, 128), *values)
        return carry

    lax.fori_loop(0, OCC // 4, combine, 0)
    multiply(lhs_ref, w_ref, sum_ref, B_BLOCK, B_STEPS, before_ref)

    label_ab = own_column(vir_ref, lax.axis_index("grp") * SEC, jnp.int32) ^ label_ref[...]

    def mask(i, carry):
        rows = pl.ds(pl.multiple_of(i % 2 * (OCC // 2 * 8) + i // 2 * 8, 8), 8)
        for j in range(OJW):
            lanes = pl.ds(j * VIR, VIR)
            keep = label_ab == (occ_ref[i] ^ occ_ref[j])
            sum_ref[rows, lanes] = jnp.where(keep, sum_ref[rows, lanes], 0.0)
        return carry

    lax.fori_loop(0, OCC, mask, 0)

    half = OWN // 2 * 8
    row = lax.broadcasted_iota(jnp.int32, (64, OWN * 8), 0)
    col = lax.broadcasted_iota(jnp.int32, (64, OWN * 8), 1)
    i, a = row // SEC, row % SEC
    dense = jnp.where((row < OWN * SEC) & (col == i % 2 * half + i // 2 * 8 + a), 1.0, 0.0).astype(BF16)
    fold = fold_ref[...]
    for s in range(CON):
        owner = lax.rem(me + s, CON)
        evens = pl.ds(pl.multiple_of(owner * half, 8), half)
        odds = pl.ds(pl.multiple_of(OCC // 2 * 8 + owner * half, 8), half)
        for j in range(OJW):
            lanes = pl.ds(j * VIR, VIR)
            value = jnp.concatenate([sum_ref[evens, lanes], sum_ref[odds, lanes]], 0)
            high = value.astype(BF16)
            parts = [(outs[s], high)]
            if s == 0:
                parts.append((outs[4], (value - high.astype(F32)).astype(BF16)))
            for out, part in parts:
                part = jnp.dot(dense, part, preferred_element_type=F32).astype(BF16)
                out[:, j * SLOT : (j + 1) * SLOT] = nt_dot(part, fold).astype(BF16)


def term_b(occ_irrep, vir_irrep, got, w, fold, before):
    return pl.pallas_call(
        term_b_kernel,
        out_shape=[jax.ShapeDtypeStruct((64, OJW * SLOT), BF16)] * 5,
        in_specs=[SMEM, SMEM] + [VMEM] * 5,
        out_specs=[VMEM] * 5,
        scratch_shapes=[
            pltpu.VMEM((OCC * OCC // 2, 8, 128), F32),
            pltpu.VMEM((B_STEPS, OCC * 8, B_BLOCK), BF16),
            pltpu.VMEM((OCC * 8, WIDE), F32),
        ],
        compiler_params=pltpu.CompilerParams(vmem_limit_bytes=14 * MIB),
        cost_estimate=pl.CostEstimate(flops=10**9, bytes_accessed=10 * 10**6, transcendentals=0),
        name="term_b",
    )(occ_irrep, vir_irrep, vir_irrep.reshape(1, VIR), got, w, fold, before)


def finish_kernel(fold_ref, scale_ref, *refs):
    chunks, out_ref = refs[:5], refs[5]
    for j in range(OJW):
        total = jnp.zeros((64, VIR), F32)
        for chunk in chunks:
            total += jnp.dot(chunk[:, j * SLOT : (j + 1) * SLOT], fold_ref[...], preferred_element_type=F32)
        for i in range(OWN):
            out_ref[i, j] = total[i * SEC : (i + 1) * SEC] * scale_ref[i, j]


def finish(fold, scale, chunks):
    return pl.pallas_call(
        finish_kernel,
        out_shape=jax.ShapeDtypeStruct((OWN, OJW, SEC, VIR), F32),
        in_specs=[VMEM] * 7,
        out_specs=VMEM,
        compiler_params=pltpu.CompilerParams(vmem_limit_bytes=8 * MIB),
        name="finish",
    )(fold, scale, *chunks)


def shards(amplitudes, integrals, occ_energy, vir_energy, occ_irrep, vir_irrep):
    x = jnp.swapaxes(amplitudes, 1, 2)
    sent_a = pack(x, A_ROWS, A_TILES, A_REST, 2, 0, A_WIDTH)
    got_a = lax.all_to_all(sent_a, "grp", split_axis=0, concat_axis=0, tiled=True)
    sent_b = pack(x, B_ROWS, B_TILES, B_REST, 4, A_WIDTH, B_WIDTH)
    got_b = lax.all_to_all(sent_b, "grp", split_axis=0, concat_axis=0, tiled=True)
    wa, wb, fold, scale = prepare(
        occ_irrep, vir_irrep, occ_energy, vir_energy, jnp.swapaxes(integrals, 1, 2)
    )
    before = term_a(got_a, wa)
    chunks = term_b(occ_irrep, vir_irrep, got_b, wb, fold, before)
    arrived = [chunks[0], chunks[4]]
    for s in (2, 1, 3):
        arrived.append(lax.ppermute(chunks[s], "con", [(n, (n + s) % CON) for n in range(CON)]))
    return finish(fold, scale, arrived)


def solution(mesh):
    return jax.shard_map(
        shards,
        mesh=mesh,
        in_specs=(P("grp", None, "con"), P(None, "con", None, None), P(), P(), P(), P()),
        out_specs=P("con", None, "grp", None),
        check_vma=False,
    )
```

```python
import jax
import jax.numpy as jnp
from jax import lax
from jax.experimental import pallas as pl
from jax.experimental.pallas import tpu as pltpu
from jax.sharding import PartitionSpec as P


OCC = 40
VIR = 384
OJW = 3
GRP = 64
CON = 4
PAIR = OCC * OCC // GRP
SEC = VIR // GRP
CW = VIR // CON
OWN = OCC // CON
SLOT = VIR // 2
WIDE = OJW * VIR
VMEM = pl.BlockSpec(memory_space=pltpu.VMEM)
SMEM = pl.BlockSpec(memory_space=pltpu.SMEM)
HBM = pl.BlockSpec(memory_space=pltpu.HBM)
MIB = 1024 * 1024
TERM_LIMIT = 50 * MIB
BF16, F32 = jnp.bfloat16, jnp.float32

COUPLES = 13
TILES = 20
GROUPS = 5
ROWS = 120
A_WIDTH, B_WIDTH = 64, 32
BLOCK = 1280
STEPS = OCC * CW // BLOCK


def nt_dot(x, y):
    return lax.dot_general(x, y, (((1,), (1,)), ((), ())), preferred_element_type=F32)


def pack_kernel(x_hbm, out_hbm, main_ref, rest_ref, pick_ref, out_ref, sem, out_sem):
    odd = lax.rem(lax.axis_index("grp"), 2)
    for t in range(TILES):
        n, j = divmod(t, 4)
        dst = rest_ref if j == 3 else main_ref.at[j]
        for p in range(2 if t < COUPLES else 4):
            if t < COUPLES:
                pair, first_c, width = 2 * t + p, 0, A_WIDTH
            else:
                pair, first_c, width = 4 * (t - COUPLES) + p, A_WIDTH, B_WIDTH
            pltpu.make_async_copy(
                x_hbm.at[jnp.clip(pair - odd, 0, PAIR - 1), pl.ds(first_c, width)],
                dst.at[pl.ds(n * 128 + p * width, width)],
                sem,
            ).start()
    row = lax.broadcasted_iota(jnp.int32, (GRP * 4, 1), 0)
    dest, sub = row // 8, row % 8
    col = lax.broadcasted_iota(jnp.int32, (GRP * 4, 256), 1)

    def pick(target):
        return jnp.where(col == target, 1.0, 0.0).astype(BF16)

    for half in range(2):
        first = dest * SEC + 64 * half
        main = pick(jnp.where(sub < 6, first + sub, -1))
        for j in range(3):
            pick_ref[half, j, :, :256] = main
            pick_ref[half, j, :, 256:] = pick(jnp.where(sub >= 6, first + 2 * j + sub - 6, -1))
    pltpu.make_async_copy(main_ref, main_ref, sem).wait()
    pltpu.make_async_copy(rest_ref, rest_ref, sem).wait()
    for j in range(3):
        for half in range(2):
            lanes = slice(128 * half, 128 * half + 256)
            both = jnp.concatenate([main_ref[j, :, lanes], rest_ref[:, lanes]], 1)
            value = nt_dot(pick_ref[half, j], both).astype(BF16)
            for n in range(GROUPS):
                tile = value[:, n * 128 : n * 128 + 128].reshape(GRP // 2, 8, 128)
                out_ref[j, half * 32 : half * 32 + 32, n * 8 : n * 8 + 8, :] = tile
        pltpu.make_async_copy(out_ref.at[j], out_hbm.at[:, pl.ds(40 * j, 40)], out_sem.at[j]).start()
    for j in range(3):
        pltpu.make_async_copy(out_ref.at[j], out_hbm.at[:, pl.ds(40 * j, 40)], out_sem.at[j]).wait()


def pack(x):
    return pl.pallas_call(
        pack_kernel,
        out_shape=jax.ShapeDtypeStruct((GRP, ROWS, 128), BF16),
        in_specs=[HBM],
        out_specs=HBM,
        scratch_shapes=[
            pltpu.VMEM((3, GROUPS * 128, VIR), BF16),
            pltpu.VMEM((GROUPS * 128, VIR), BF16),
            pltpu.VMEM((2, 3, GRP * 4, 512), BF16),
            pltpu.VMEM((3, GRP, 40, 128), BF16),
            pltpu.SemaphoreType.DMA,
            pltpu.SemaphoreType.DMA((3,)),
        ],
        compiler_params=pltpu.CompilerParams(vmem_limit_bytes=62 * MIB),
        name="pack",
    )(x)


def own_column(ref, first, dtype):
    row = lax.broadcasted_iota(jnp.int32, (8, 1), 0)
    column = jnp.zeros((8, 1), dtype)
    for a in range(SEC):
        column = jnp.where(row == a, ref[first + a], column)
    return column


def prepare_kernel(
    occ_ref, vir_ref, occ_e_ref, vir_e_ref, label_ref, energy_ref, w_hbm, w_ref, fold_ref, scale_ref, sem
):
    def fetch(kq, carry):
        for n in range(4):
            for j in range(OJW):
                source = w_hbm.at[4 * kq + n, j]
                lanes = pl.ds(j * VIR, VIR)
                at_a = pl.multiple_of(kq * 256 + n * A_WIDTH, A_WIDTH)
                at_b = pl.multiple_of(OCC * A_WIDTH + kq * 128 + n * B_WIDTH, B_WIDTH)
                pltpu.make_async_copy(
                    source.at[pl.ds(0, A_WIDTH)], w_ref.at[pl.ds(at_a, A_WIDTH), lanes], sem
                ).start()
                pltpu.make_async_copy(
                    source.at[pl.ds(A_WIDTH, B_WIDTH)], w_ref.at[pl.ds(at_b, B_WIDTH), lanes], sem
                ).start()
        return carry

    lax.fori_loop(0, 10, fetch, 0)

    labels = label_ref[...]
    label_row = labels.astype(F32)
    label_col = jnp.transpose(jnp.broadcast_to(label_row, (8, VIR)))[:, :1]
    first = lax.broadcasted_iota(jnp.int32, (VIR, VIR), 0)
    second = lax.broadcasted_iota(jnp.int32, (VIR, VIR), 1)
    ahead = (label_col < label_row) | ((label_col == label_row) & (first < second))
    rank = jnp.sum(jnp.where(ahead, 1.0, 0.0), axis=0, keepdims=True)
    slot = jnp.where(rank >= SLOT, rank - SLOT, rank).astype(jnp.int32)
    fold_ref[...] = jnp.where(lax.broadcasted_iota(jnp.int32, (SLOT, VIR), 0) == slot, 1.0, 0.0).astype(BF16)

    own_i, own_a = lax.axis_index("con") * OWN, lax.axis_index("grp") * SEC
    label_ab = (own_column(vir_ref, own_a, jnp.int32) ^ labels)[:SEC]
    energy_ab = (own_column(vir_e_ref, own_a, F32) + energy_ref[...])[:SEC]
    for i in range(OWN):
        for j in range(OJW):
            keep = label_ab == (occ_ref[own_i + i] ^ occ_ref[j])
            denominator = occ_e_ref[own_i + i] + occ_e_ref[j] - energy_ab
            scale_ref[i, j] = jnp.where(keep, 1.0, 0.0) / denominator

    pltpu.make_async_copy(w_ref, w_ref, sem).wait()


def prepare(occ_irrep, vir_irrep, occ_energy, vir_energy, w):
    return pl.pallas_call(
        prepare_kernel,
        out_shape=[
            jax.ShapeDtypeStruct((OCC * CW, WIDE), BF16),
            jax.ShapeDtypeStruct((SLOT, VIR), BF16),
            jax.ShapeDtypeStruct((OWN, OJW, SEC, VIR), F32),
        ],
        in_specs=[SMEM] * 4 + [VMEM] * 2 + [HBM],
        out_specs=[VMEM] * 3,
        scratch_shapes=[pltpu.SemaphoreType.DMA],
        compiler_params=pltpu.CompilerParams(vmem_limit_bytes=24 * MIB),
        cost_estimate=pl.CostEstimate(flops=10**8, bytes_accessed=20 * 10**6, transcendentals=0),
        name="prepare",
    )(
        occ_irrep,
        vir_irrep,
        occ_energy,
        vir_energy,
        vir_irrep.reshape(1, VIR),
        vir_energy.reshape(1, VIR),
        w,
    )


def lane_tiles(got_ref, s):
    got = got_ref[s].astype(F32).reshape(ROWS // 8, 8, 128)
    sub = lax.broadcasted_iota(jnp.int32, (8, 128), 0)
    tiles = []
    for t in range(TILES):
        n, j = divmod(t, 4)
        if j < 3:
            tiles.append(got[GROUPS * j + n])
        else:
            a, b, c = (pltpu.roll(got[GROUPS * j + n], 2 + 2 * j, 0) for j in range(3))
            tiles.append(jnp.where(sub < 2, a, jnp.where(sub < 4, b, c)))
    return tiles


def store_couples(h, even, odd, half, couple_ref):
    lane = lax.broadcasted_iota(jnp.int32, (8, 128), 1)
    for u in range(COUPLES - 1):
        couple_ref[PAIR * h + u] = even[u]
        couple_ref[PAIR * h + COUPLES + u] = odd[u + 1]
    couple_ref[PAIR * h + COUPLES - 1] = jnp.where(lane < half, even[COUPLES - 1], odd[0])


def term_kernel(occ_ref, vir_ref, label_ref, got_ref, fold_ref, w_hbm, *refs):
    outs, own_ref, refs = refs[:3], refs[3], refs[4:]
    a_ref, b_ref, w_ref, sum_ref, masked_ref, sems = refs[:6]
    lhs_refs = refs[6:]
    me = lax.axis_index("con")
    half = OCC // 2 * 8

    def fetch(step):
        return pltpu.make_async_copy(w_hbm.at[pl.ds(step * BLOCK, BLOCK)], w_ref.at[step], sems.at[step])

    for step in range(STEPS):
        fetch(step).start()

    def unpack(h, carry):
        units_a, units_b = [], []
        for n in range(2):
            tiles = lane_tiles(got_ref, 2 * h + n)
            units_a.append(tiles[:COUPLES])
            units_b.append([
                tiles[COUPLES + u // 2] if u % 2 == 0 else pltpu.roll(tiles[COUPLES + u // 2], 64, 1)
                for u in range(COUPLES)
            ])
        store_couples(h, *units_a, 64, a_ref)
        store_couples(h, *units_b, 32, b_ref)
        return carry

    lax.fori_loop(0, GRP // 2, unpack, 0)

    lane = lax.broadcasted_iota(jnp.int32, (OCC // 2, 8, 128), 2)
    a_by_i, a_by_parity = a_ref.reshape(OCC, OCC // 2, 8, 128), a_ref.reshape(OCC // 2, 2, OCC // 2, 8, 128)
    b_by_i, b_by_parity = b_ref.reshape(OCC, OCC // 2, 8, 128), b_ref.reshape(OCC // 2, 2, OCC // 2, 8, 128)

    def combine_a(kk):
        first, second = a_by_i[2 * kk], a_by_i[2 * kk + 1]
        even = jnp.where(lane < 64, first, pltpu.roll(second, 64, 2))
        odd = jnp.where(lane < 64, pltpu.roll(first, 64, 2), second)
        return 2.0 * a_by_parity[:, 0, kk] - even, 2.0 * a_by_parity[:, 1, kk] - odd

    def combine_b(kq):
        crossed = [b_by_i[4 * kq + n] for n in range(4)]
        values = []
        for parity in range(2):
            part = [
                crossed[n] if n == parity else pltpu.roll(crossed[n], 32 * (n - parity) % 128, 2) for n in range(4)
            ]
            low, high = jnp.where(lane < 32, part[0], part[1]), jnp.where(lane < 96, part[2], part[3])
            direct = jnp.where(
                lane < 64, b_by_parity[:, parity, 2 * kq], pltpu.roll(b_by_parity[:, parity, 2 * kq + 1], 64, 2)
            )
            values.append(2.0 * direct - jnp.where(lane < 64, low, high))
        return values

    def combine(step):
        def body(n, carry):
            even, odd = combine_a(step * 10 + n) if step < 2 else combine_b(n)
            lanes = pl.ds(pl.multiple_of(n * 128, 128), 128)
            lhs_refs[step][:half, lanes] = even.reshape(half, 128).astype(BF16)
            lhs_refs[step][half:, lanes] = odd.reshape(half, 128).astype(BF16)
            return carry

        lax.fori_loop(0, 10, body, 0)

    for step in range(STEPS):
        combine(step)
        fetch(step).wait()
        part = jnp.dot(lhs_refs[step][...], w_ref[step], preferred_element_type=F32)
        sum_ref[...] = part if step == 0 else sum_ref[...] + part

    label_ab = own_column(vir_ref, lax.axis_index("grp") * SEC, jnp.int32) ^ label_ref[...]
    small = OWN // 2 * 8
    row = lax.broadcasted_iota(jnp.int32, (64, OWN * 8), 0)
    col = lax.broadcasted_iota(jnp.int32, (64, OWN * 8), 1)
    i, a = row // SEC, row % SEC
    dense = jnp.where((row < OWN * SEC) & (col == i % 2 * small + i // 2 * 8 + a), 1.0, 0.0).astype(BF16)
    for s in range(CON):
        owner = lax.rem(me + s, CON)
        for n in range(OWN):
            place = n % 2 * small + n // 2 * 8
            rows = pl.ds(pl.multiple_of(n % 2 * half + owner * small + n // 2 * 8, 8), 8)
            if s == 0:
                own_ref[place : place + 8, :] = sum_ref[rows, :]
                continue
            for j in range(OJW):
                keep = label_ab == (occ_ref[owner * OWN + n] ^ occ_ref[j])
                masked_ref[j * OWN * 8 + place : j * OWN * 8 + place + 8, :] = jnp.where(
                    keep, sum_ref[rows, j * VIR : (j + 1) * VIR], 0.0
                )
        if s > 0:
            folded = nt_dot(masked_ref[...].astype(BF16), fold_ref[...]).astype(BF16)
            for j in range(OJW):
                chunk = jnp.dot(dense, folded[j * OWN * 8 : (j + 1) * OWN * 8], preferred_element_type=F32)
                outs[s - 1][:, j * SLOT : (j + 1) * SLOT] = chunk.astype(BF16)


def term(occ_irrep, vir_irrep, got, fold, w):
    return pl.pallas_call(
        term_kernel,
        out_shape=[jax.ShapeDtypeStruct((64, OJW * SLOT), BF16)] * 3
        + [jax.ShapeDtypeStruct((OWN * 8, WIDE), F32)],
        in_specs=[SMEM, SMEM] + [VMEM] * 3 + [HBM],
        out_specs=[VMEM] * 4,
        scratch_shapes=[
            pltpu.VMEM((OCC * OCC // 2, 8, 128), F32),
            pltpu.VMEM((OCC * OCC // 2, 8, 128), F32),
            pltpu.VMEM((STEPS, BLOCK, WIDE), BF16),
            pltpu.VMEM((OCC * 8, WIDE), F32),
            pltpu.VMEM((OJW * OWN * 8, VIR), F32),
            pltpu.SemaphoreType.DMA((STEPS,)),
        ]
        + [pltpu.VMEM((OCC * 8, BLOCK), BF16)] * STEPS,
        compiler_params=pltpu.CompilerParams(vmem_limit_bytes=TERM_LIMIT),
        name="term",
    )(occ_irrep, vir_irrep, vir_irrep.reshape(1, VIR), got, fold, w)


def finish_kernel(fold_ref, scale_ref, own_ref, *refs):
    chunks, out_ref = refs[:3], refs[3]
    for j in range(OJW):
        lanes = slice(j * SLOT, (j + 1) * SLOT)
        stacked = jnp.concatenate([chunk[:, lanes] for chunk in chunks], 0)
        parts = jnp.dot(stacked, fold_ref[...], preferred_element_type=F32)
        total = parts[:64] + parts[64:128] + parts[128:]
        for i in range(OWN):
            place = i % 2 * (OWN // 2 * 8) + i // 2 * 8
            own = own_ref[place : place + SEC, j * VIR : (j + 1) * VIR]
            out_ref[i, j] = (own + total[i * SEC : (i + 1) * SEC]) * scale_ref[i, j]


def finish(fold, scale, own, chunks):
    return pl.pallas_call(
        finish_kernel,
        out_shape=jax.ShapeDtypeStruct((OWN, OJW, SEC, VIR), F32),
        in_specs=[VMEM] * 6,
        out_specs=VMEM,
        compiler_params=pltpu.CompilerParams(vmem_limit_bytes=8 * MIB),
        name="finish",
    )(fold, scale, own, *chunks)


def shards(amplitudes, integrals, occ_energy, vir_energy, occ_irrep, vir_irrep):
    sent = pack(jnp.swapaxes(amplitudes, 1, 2))
    got = lax.all_to_all(sent, "grp", split_axis=0, concat_axis=0, tiled=True)
    w, fold, scale = prepare(
        occ_irrep, vir_irrep, occ_energy, vir_energy, jnp.swapaxes(integrals, 1, 2)
    )
    *chunks, own = term(occ_irrep, vir_irrep, got, fold, w)
    arrived = [lax.ppermute(chunks[s - 1], "con", [(n, (n + s) % CON) for n in range(CON)]) for s in (2, 1, 3)]
    return finish(fold, scale, own, arrived)


def solution(mesh):
    return jax.shard_map(
        shards,
        mesh=mesh,
        in_specs=(P("grp", None, "con"), P(None, "con", None, None), P(), P(), P(), P()),
        out_specs=P("con", None, "grp", None),
        check_vma=False,
    )
```

```python
import jax
import jax.numpy as jnp
from jax import lax
from jax.experimental import pallas as pl
from jax.experimental.pallas import tpu as pltpu
from jax.sharding import PartitionSpec as P


OCC = 40
VIR = 384
OJW = 3
GRP = 64
CON = 4
PAIR = OCC * OCC // GRP
SEC = VIR // GRP
CW = VIR // CON
OWN = OCC // CON
SLOT = VIR // 2
WIDE = OJW * VIR
VMEM = pl.BlockSpec(memory_space=pltpu.VMEM)
SMEM = pl.BlockSpec(memory_space=pltpu.SMEM)
HBM = pl.BlockSpec(memory_space=pltpu.HBM)
MIB = 1024 * 1024
TERM_LIMIT = 50 * MIB
BF16, F32 = jnp.bfloat16, jnp.float32

COUPLES = 13
TILES = 20
GROUPS = 5
ROWS = 120
A_WIDTH, B_WIDTH = 64, 32
BLOCK = 1280
STEPS = OCC * CW // BLOCK


def nt_dot(x, y):
    return lax.dot_general(x, y, (((1,), (1,)), ((), ())), preferred_element_type=F32)


def pack_kernel(x_hbm, out_hbm, main_ref, rest_ref, pick_ref, out_ref, sem, out_sem):
    me = lax.axis_index("grp")
    odd, phase = lax.rem(me, 2), lax.rem(me, 4)
    for t in range(TILES):
        n, j = divmod(t, 4)
        dst = rest_ref if j == 3 else main_ref.at[j]
        for p in range(2 if t < COUPLES else 4):
            if t < COUPLES:
                pair, first_c, width = 2 * t + p - odd, 0, A_WIDTH
            else:
                pair, first_c, width = 4 * (t - COUPLES) + p - phase, A_WIDTH, B_WIDTH
            pltpu.make_async_copy(
                x_hbm.at[jnp.clip(pair, 0, PAIR - 1), pl.ds(first_c, width)],
                dst.at[pl.ds(n * 128 + p * width, width)],
                sem,
            ).start()
    row = lax.broadcasted_iota(jnp.int32, (GRP * 4, 1), 0)
    dest, sub = row // 8, row % 8
    col = lax.broadcasted_iota(jnp.int32, (GRP * 4, 256), 1)

    def pick(target):
        return jnp.where(col == target, 1.0, 0.0).astype(BF16)

    for half in range(2):
        first = dest * SEC + 64 * half
        main = pick(jnp.where(sub < 6, first + sub, -1))
        for j in range(3):
            pick_ref[half, j, :, :256] = main
            pick_ref[half, j, :, 256:] = pick(jnp.where(sub >= 6, first + 2 * j + sub - 6, -1))
    pltpu.make_async_copy(main_ref, main_ref, sem).wait()
    pltpu.make_async_copy(rest_ref, rest_ref, sem).wait()
    for j in range(3):
        for half in range(2):
            lanes = slice(128 * half, 128 * half + 256)
            both = jnp.concatenate([main_ref[j, :, lanes], rest_ref[:, lanes]], 1)
            value = nt_dot(pick_ref[half, j], both).astype(BF16)
            for n in range(GROUPS):
                tile = value[:, n * 128 : n * 128 + 128].reshape(GRP // 2, 8, 128)
                out_ref[j, half * 32 : half * 32 + 32, n * 8 : n * 8 + 8, :] = tile
        pltpu.make_async_copy(out_ref.at[j], out_hbm.at[:, pl.ds(40 * j, 40)], out_sem.at[j]).start()
    for j in range(3):
        pltpu.make_async_copy(out_ref.at[j], out_hbm.at[:, pl.ds(40 * j, 40)], out_sem.at[j]).wait()


def pack(x):
    return pl.pallas_call(
        pack_kernel,
        out_shape=jax.ShapeDtypeStruct((GRP, ROWS, 128), BF16),
        in_specs=[HBM],
        out_specs=HBM,
        scratch_shapes=[
            pltpu.VMEM((3, GROUPS * 128, VIR), BF16),
            pltpu.VMEM((GROUPS * 128, VIR), BF16),
            pltpu.VMEM((2, 3, GRP * 4, 512), BF16),
            pltpu.VMEM((3, GRP, 40, 128), BF16),
            pltpu.SemaphoreType.DMA,
            pltpu.SemaphoreType.DMA((3,)),
        ],
        compiler_params=pltpu.CompilerParams(vmem_limit_bytes=62 * MIB),
        name="pack",
    )(x)


def own_column(ref, first, dtype):
    row = lax.broadcasted_iota(jnp.int32, (8, 1), 0)
    column = jnp.zeros((8, 1), dtype)
    for a in range(SEC):
        column = jnp.where(row == a, ref[first + a], column)
    return column


def prepare_kernel(
    occ_ref, vir_ref, occ_e_ref, vir_e_ref, label_ref, energy_ref, w_hbm, w_ref, fold_ref, scale_ref, sem
):
    def fetch(kq, carry):
        for n in range(4):
            for j in range(OJW):
                source = w_hbm.at[4 * kq + n, j]
                lanes = pl.ds(j * VIR, VIR)
                at_a = pl.multiple_of(kq * 256 + n * A_WIDTH, A_WIDTH)
                at_b = pl.multiple_of(OCC * A_WIDTH + kq * 128 + n * B_WIDTH, B_WIDTH)
                pltpu.make_async_copy(
                    source.at[pl.ds(0, A_WIDTH)], w_ref.at[pl.ds(at_a, A_WIDTH), lanes], sem
                ).start()
                pltpu.make_async_copy(
                    source.at[pl.ds(A_WIDTH, B_WIDTH)], w_ref.at[pl.ds(at_b, B_WIDTH), lanes], sem
                ).start()
        return carry

    lax.fori_loop(0, 10, fetch, 0)

    labels = label_ref[...]
    label_row = labels.astype(F32)
    label_col = jnp.transpose(jnp.broadcast_to(label_row, (8, VIR)))[:, :1]
    first = lax.broadcasted_iota(jnp.int32, (VIR, VIR), 0)
    second = lax.broadcasted_iota(jnp.int32, (VIR, VIR), 1)
    ahead = (label_col < label_row) | ((label_col == label_row) & (first < second))
    rank = jnp.sum(jnp.where(ahead, 1.0, 0.0), axis=0, keepdims=True)
    slot = jnp.where(rank >= SLOT, rank - SLOT, rank).astype(jnp.int32)
    fold_ref[...] = jnp.where(lax.broadcasted_iota(jnp.int32, (SLOT, VIR), 0) == slot, 1.0, 0.0).astype(BF16)

    own_i, own_a = lax.axis_index("con") * OWN, lax.axis_index("grp") * SEC
    label_ab = (own_column(vir_ref, own_a, jnp.int32) ^ labels)[:SEC]
    energy_ab = (own_column(vir_e_ref, own_a, F32) + energy_ref[...])[:SEC]
    for i in range(OWN):
        for j in range(OJW):
            keep = label_ab == (occ_ref[own_i + i] ^ occ_ref[j])
            denominator = occ_e_ref[own_i + i] + occ_e_ref[j] - energy_ab
            scale_ref[i, j] = jnp.where(keep, 1.0, 0.0) / denominator

    pltpu.make_async_copy(w_ref, w_ref, sem).wait()


def prepare(occ_irrep, vir_irrep, occ_energy, vir_energy, w):
    return pl.pallas_call(
        prepare_kernel,
        out_shape=[
            jax.ShapeDtypeStruct((OCC * CW, WIDE), BF16),
            jax.ShapeDtypeStruct((SLOT, VIR), BF16),
            jax.ShapeDtypeStruct((OWN, OJW, SEC, VIR), F32),
        ],
        in_specs=[SMEM] * 4 + [VMEM] * 2 + [HBM],
        out_specs=[VMEM] * 3,
        scratch_shapes=[pltpu.SemaphoreType.DMA],
        compiler_params=pltpu.CompilerParams(vmem_limit_bytes=24 * MIB),
        cost_estimate=pl.CostEstimate(flops=10**8, bytes_accessed=20 * 10**6, transcendentals=0),
        name="prepare",
    )(
        occ_irrep,
        vir_irrep,
        occ_energy,
        vir_energy,
        vir_irrep.reshape(1, VIR),
        vir_energy.reshape(1, VIR),
        w,
    )


def lane_tiles(got_ref, s):
    got = got_ref[s].astype(F32).reshape(ROWS // 8, 8, 128)
    sub = lax.broadcasted_iota(jnp.int32, (8, 128), 0)
    tiles = []
    for t in range(TILES):
        n, j = divmod(t, 4)
        if j < 3:
            tiles.append(got[GROUPS * j + n])
        else:
            a, b, c = (pltpu.roll(got[GROUPS * j + n], 2 + 2 * j, 0) for j in range(3))
            tiles.append(jnp.where(sub < 2, a, jnp.where(sub < 4, b, c)))
    return tiles


def term_kernel(occ_ref, vir_ref, label_ref, got_ref, fold_ref, w_hbm, *refs):
    outs, own_ref, refs = refs[:3], refs[3], refs[4:]
    a_ref, b_ref, w_ref, sum_ref, masked_ref, sems = refs[:6]
    lhs_refs = refs[6:]
    me = lax.axis_index("con")

    def fetch(step):
        return pltpu.make_async_copy(w_hbm.at[pl.ds(step * BLOCK, BLOCK)], w_ref.at[step], sems.at[step])

    for step in range(STEPS):
        fetch(step).start()

    lane2 = lax.broadcasted_iota(jnp.int32, (8, 128), 1)

    def unpack(h, carry):
        last_a = last_b = None
        for n in range(4):
            tiles = lane_tiles(got_ref, 4 * h + n)
            units_a, units_b = tiles[:COUPLES], tiles[COUPLES:]
            if n % 2:
                units_a[0] = jnp.where(lane2 < 64, last_a, units_a[0])
            if n > 0:
                units_b[0] = jnp.where(lane2 < 32 * n, last_b, units_b[0])
            last_a, last_b = units_a[-1], units_b[-1]
            for u in range(COUPLES if n % 2 else COUPLES - 1):
                a_ref[50 * h + 25 * n // 2 + u] = units_a[u]
            for u in range(7 if n == 3 else 6):
                b_ref[25 * h + 6 * n + u] = units_b[u]
        return carry

    lax.fori_loop(0, GRP // 4, unpack, 0)

    ten = OCC // 4
    lane = lax.broadcasted_iota(jnp.int32, (OCC // 2, 8, 128), 2)
    lane_b = lax.broadcasted_iota(jnp.int32, (ten, 8, 128), 2)
    a_by_i, a_by_m = a_ref.reshape(OCC, OCC // 2, 8, 128), a_ref.reshape(ten, 4, OCC // 2, 8, 128)
    b_by_i, b_by_m = b_ref.reshape(OCC, ten, 8, 128), b_ref.reshape(ten, 4, ten, 8, 128)

    def crossed_a(kk):
        first, second = a_by_i[2 * kk], a_by_i[2 * kk + 1]
        even = jnp.where(lane < 64, first, pltpu.roll(second, 64, 2)).reshape(ten, 2, 8, 128)
        odd = jnp.where(lane < 64, pltpu.roll(first, 64, 2), second).reshape(ten, 2, 8, 128)
        return even[:, 0], odd[:, 0], even[:, 1], odd[:, 1]

    def crossed_b(kq):
        c = [b_by_i[4 * kq + n] for n in range(4)]
        low, upper = lane_b < 64, lane_b % 64 >= 32
        wide = []
        for n in range(2):
            wide.append(jnp.where(low, c[n], pltpu.roll(c[n + 2], 64, 2)))
        for n in range(2):
            wide.append(jnp.where(low, pltpu.roll(c[n], 64, 2), c[n + 2]))
        found = []
        for m in (0, 2):
            found.append(jnp.where(upper, pltpu.roll(wide[m + 1], 32, 2), wide[m]))
            found.append(jnp.where(upper, wide[m + 1], pltpu.roll(wide[m], 96, 2)))
        return found

    def combine(step, n, lanes):
        if step < 2:
            by_m, k, crossed = a_by_m, step * 10 + n, crossed_a(step * 10 + n)
        else:
            by_m, k, crossed = b_by_m, n, crossed_b(n)
        for m in range(4):
            value = 2.0 * by_m[:, m, k] - crossed[m]
            lhs_refs[step][m * ten * 8 : (m + 1) * ten * 8, lanes] = value.reshape(ten * 8, 128).astype(BF16)

    def combine_first(n, carry):
        combine(0, n, pl.ds(pl.multiple_of(n * 128, 128), 128))
        return carry

    lax.fori_loop(0, 10, combine_first, 0)
    for step in range(STEPS):
        fetch(step).wait()
        if step + 1 < STEPS:
            for n in range(10):
                combine(step + 1, n, slice(n * 128, n * 128 + 128))
        part = jnp.dot(lhs_refs[step][...], w_ref[step], preferred_element_type=F32)
        sum_ref[...] = part if step == 0 else sum_ref[...] + part

    label_ab = own_column(vir_ref, lax.axis_index("grp") * SEC, jnp.int32) ^ label_ref[...]
    row = lax.broadcasted_iota(jnp.int32, (64, OWN * 8), 0)
    col = lax.broadcasted_iota(jnp.int32, (64, OWN * 8), 1)
    dense = jnp.where((row < OWN * SEC) & (col == row // SEC * 8 + row % SEC), 1.0, 0.0).astype(BF16)
    for s in range(CON):
        owner = lax.rem(me + s, CON)
        for n in range(OWN):
            i = owner * OWN + n
            rows = pl.ds(pl.multiple_of((lax.rem(i, 4) * ten + lax.div(i, 4)) * 8, 8), 8)
            if s == 0:
                own_ref[n * 8 : n * 8 + 8, :] = sum_ref[rows, :]
                continue
            for j in range(OJW):
                keep = label_ab == (occ_ref[i] ^ occ_ref[j])
                at = (j * OWN + n) * 8
                masked_ref[at : at + 8, :] = jnp.where(keep, sum_ref[rows, j * VIR : (j + 1) * VIR], 0.0)
        if s > 0:
            folded = nt_dot(masked_ref[...].astype(BF16), fold_ref[...]).astype(BF16)
            for j in range(OJW):
                chunk = jnp.dot(dense, folded[j * OWN * 8 : (j + 1) * OWN * 8], preferred_element_type=F32)
                outs[s - 1][:, j * SLOT : (j + 1) * SLOT] = chunk.astype(BF16)


def term(occ_irrep, vir_irrep, got, fold, w):
    return pl.pallas_call(
        term_kernel,
        out_shape=[jax.ShapeDtypeStruct((64, OJW * SLOT), BF16)] * 3
        + [jax.ShapeDtypeStruct((OWN * 8, WIDE), F32)],
        in_specs=[SMEM, SMEM] + [VMEM] * 3 + [HBM],
        out_specs=[VMEM] * 4,
        scratch_shapes=[
            pltpu.VMEM((OCC * OCC // 2, 8, 128), F32),
            pltpu.VMEM((OCC * OCC // 4, 8, 128), F32),
            pltpu.VMEM((STEPS, BLOCK, WIDE), BF16),
            pltpu.VMEM((OCC * 8, WIDE), F32),
            pltpu.VMEM((OJW * OWN * 8, VIR), F32),
            pltpu.SemaphoreType.DMA((STEPS,)),
        ]
        + [pltpu.VMEM((OCC * 8, BLOCK), BF16)] * STEPS,
        compiler_params=pltpu.CompilerParams(vmem_limit_bytes=TERM_LIMIT),
        name="term",
    )(occ_irrep, vir_irrep, vir_irrep.reshape(1, VIR), got, fold, w)


def finish_kernel(fold_ref, scale_ref, own_ref, *refs):
    chunks, out_ref = refs[:3], refs[3]
    for j in range(OJW):
        lanes = slice(j * SLOT, (j + 1) * SLOT)
        stacked = jnp.concatenate([chunk[:, lanes] for chunk in chunks], 0)
        parts = jnp.dot(stacked, fold_ref[...], preferred_element_type=F32)
        total = parts[:64] + parts[64:128] + parts[128:]
        for i in range(OWN):
            own = own_ref[i * 8 : i * 8 + SEC, j * VIR : (j + 1) * VIR]
            out_ref[i, j] = (own + total[i * SEC : (i + 1) * SEC]) * scale_ref[i, j]


def finish(fold, scale, own, chunks):
    return pl.pallas_call(
        finish_kernel,
        out_shape=jax.ShapeDtypeStruct((OWN, OJW, SEC, VIR), F32),
        in_specs=[VMEM] * 6,
        out_specs=VMEM,
        compiler_params=pltpu.CompilerParams(vmem_limit_bytes=8 * MIB),
        name="finish",
    )(fold, scale, own, *chunks)


def shards(amplitudes, integrals, occ_energy, vir_energy, occ_irrep, vir_irrep):
    sent = pack(jnp.swapaxes(amplitudes, 1, 2))
    got = lax.all_to_all(sent, "grp", split_axis=0, concat_axis=0, tiled=True)
    w, fold, scale = prepare(
        occ_irrep, vir_irrep, occ_energy, vir_energy, jnp.swapaxes(integrals, 1, 2)
    )
    *chunks, own = term(occ_irrep, vir_irrep, got, fold, w)
    arrived = [lax.ppermute(chunks[s - 1], "con", [(n, (n + s) % CON) for n in range(CON)]) for s in (2, 1, 3)]
    return finish(fold, scale, own, arrived)


def solution(mesh):
    return jax.shard_map(
        shards,
        mesh=mesh,
        in_specs=(P("grp", None, "con"), P(None, "con", None, None), P(), P(), P(), P()),
        out_specs=P("con", None, "grp", None),
        check_vma=False,
    )
```

```python
import jax
import jax.numpy as jnp
from jax import lax
from jax.experimental import pallas as pl
from jax.experimental.pallas import tpu as pltpu
from jax.sharding import PartitionSpec as P


OCC = 40
VIR = 384
OJW = 3
GRP = 64
CON = 4
PAIR = OCC * OCC // GRP
SEC = VIR // GRP
CW = VIR // CON
OWN = OCC // CON
SLOT = VIR // 2
WIDE = OJW * VIR
VMEM = pl.BlockSpec(memory_space=pltpu.VMEM)
SMEM = pl.BlockSpec(memory_space=pltpu.SMEM)
HBM = pl.BlockSpec(memory_space=pltpu.HBM)
MIB = 1024 * 1024
TERM_LIMIT = 50 * MIB
BF16, F32 = jnp.bfloat16, jnp.float32

COUPLES = 13
TILES = 20
ROWS = 120
CHUNK = 288
A_WIDTH, B_WIDTH = 64, 32
BLOCK = 1280
STEPS = OCC * CW // BLOCK


def nt_dot(x, y):
    return lax.dot_general(x, y, (((1,), (1,)), ((), ())), preferred_element_type=F32)


def pack_kernel(x_hbm, out_hbm, x_ref, tile_ref, pick_ref, out_ref, sem, out_sem):
    me = lax.axis_index("grp")
    odd, phase = lax.rem(me, 2), lax.rem(me, 4)
    arrivals = []
    for step, (first, last, first_c, last_c) in enumerate(PIECES):
        part = (pl.ds(first, last - first), pl.ds(first_c, last_c - first_c))
        arrivals.append(pltpu.make_async_copy(x_hbm.at[part], x_ref.at[part], sem.at[step]))
        arrivals[-1].start()
    row = lax.broadcasted_iota(jnp.int32, (GRP * 4, 1), 0)
    dest, sub = row // 8, row % 8
    col = lax.broadcasted_iota(jnp.int32, (GRP * 4, 256), 1)

    def pick(target):
        return jnp.where(col == target, 1.0, 0.0).astype(BF16)

    for half in range(2):
        first = dest * SEC + 64 * half
        main = pick(jnp.where(sub < 6, first + sub, -1))
        for j in range(3):
            pick_ref[half, j, :, :256] = main
            pick_ref[half, j, :, 256:] = pick(jnp.where(sub >= 6, first + 2 * j + sub - 6, -1))

    def place(t, at):
        for p in range(2 if t < COUPLES else 4):
            if t < COUPLES:
                pair, first_c, width = 2 * t + p - odd, 0, A_WIDTH
            else:
                pair, first_c, width = 4 * (t - COUPLES) + p - phase, A_WIDTH, B_WIDTH
            source = x_ref[jnp.clip(pair, 0, PAIR - 1), first_c : first_c + width, :]
            tile_ref[at + p * width : at + (p + 1) * width, :] = source

    sends = []
    for step, groups in enumerate(PACK_STEPS):
        if step < len(arrivals):
            arrivals[step].wait()
        size = 128 * len(groups)
        for n, group in enumerate(groups):
            for j in range(4):
                place(4 * group + j, (4 * step + j) * 256 + n * 128)
        for j in range(3):
            main, rest = (slice((4 * step + m) * 256, (4 * step + m) * 256 + size) for m in (j, 3))
            for half in range(2):
                lanes = slice(128 * half, 128 * half + 256)
                both = jnp.concatenate([tile_ref[main, lanes], tile_ref[rest, lanes]], 1)
                value = nt_dot(pick_ref[half, j], both).astype(BF16)
                for n, group in enumerate(groups):
                    tile = value[:, n * 128 : n * 128 + 128].reshape(GRP // 2, 8, 128)
                    at = (3 * group + j) * 8
                    out_ref[half * 32 : half * 32 + 32, at : at + 8, :] = tile
        rows = pl.ds(24 * groups[0], 24 * len(groups))
        sends.append(pltpu.make_async_copy(out_ref.at[:, rows], out_hbm.at[:, rows], out_sem.at[step]))
        sends[-1].start()
    for send in sends:
        send.wait()


PACK_STEPS = ((0,), (1, 2), (3, 4))
PIECES = ((0, 8, 0, A_WIDTH), (8, PAIR, 0, A_WIDTH), (0, PAIR, A_WIDTH, CW))


def pack(x):
    return pl.pallas_call(
        pack_kernel,
        out_shape=jax.ShapeDtypeStruct((GRP, ROWS, 128), BF16),
        in_specs=[HBM],
        out_specs=HBM,
        scratch_shapes=[
            pltpu.VMEM((PAIR, CW, VIR), BF16),
            pltpu.VMEM((len(PACK_STEPS) * 4 * 256, VIR), BF16),
            pltpu.VMEM((2, 3, GRP * 4, 512), BF16),
            pltpu.VMEM((GRP, ROWS, 128), BF16),
            pltpu.SemaphoreType.DMA((len(PIECES),)),
            pltpu.SemaphoreType.DMA((len(PACK_STEPS),)),
        ],
        compiler_params=pltpu.CompilerParams(vmem_limit_bytes=62 * MIB),
        name="pack",
    )(x)


def own_column(ref, first, dtype):
    row = lax.broadcasted_iota(jnp.int32, (8, 1), 0)
    column = jnp.zeros((8, 1), dtype)
    for a in range(SEC):
        column = jnp.where(row == a, ref[first + a], column)
    return column


def prepare_kernel(
    occ_ref, vir_ref, occ_e_ref, vir_e_ref, label_ref, energy_ref, w_hbm, w_ref, fold_ref, scale_ref, sem
):
    def fetch(kq, carry):
        for n in range(4):
            for j in range(OJW):
                source = w_hbm.at[4 * kq + n, j]
                lanes = pl.ds(j * VIR, VIR)
                at_a = pl.multiple_of(kq * 256 + n * A_WIDTH, A_WIDTH)
                at_b = pl.multiple_of(OCC * A_WIDTH + kq * 128 + n * B_WIDTH, B_WIDTH)
                pltpu.make_async_copy(
                    source.at[pl.ds(0, A_WIDTH)], w_ref.at[pl.ds(at_a, A_WIDTH), lanes], sem
                ).start()
                pltpu.make_async_copy(
                    source.at[pl.ds(A_WIDTH, B_WIDTH)], w_ref.at[pl.ds(at_b, B_WIDTH), lanes], sem
                ).start()
        return carry

    lax.fori_loop(0, 10, fetch, 0)

    labels = label_ref[...]
    label_row = labels.astype(F32)
    label_col = jnp.transpose(jnp.broadcast_to(label_row, (8, VIR)))[:, :1]
    first = lax.broadcasted_iota(jnp.int32, (VIR, VIR), 0)
    second = lax.broadcasted_iota(jnp.int32, (VIR, VIR), 1)
    ahead = (label_col < label_row) | ((label_col == label_row) & (first < second))
    rank = jnp.sum(jnp.where(ahead, 1.0, 0.0), axis=0, keepdims=True)
    slot = jnp.where(rank >= SLOT, rank - SLOT, rank).astype(jnp.int32)
    fold_ref[...] = jnp.where(lax.broadcasted_iota(jnp.int32, (SLOT, VIR), 0) == slot, 1.0, 0.0).astype(BF16)

    own_i, own_a = lax.axis_index("con") * OWN, lax.axis_index("grp") * SEC
    label_ab = (own_column(vir_ref, own_a, jnp.int32) ^ labels)[:SEC]
    energy_ab = (own_column(vir_e_ref, own_a, F32) + energy_ref[...])[:SEC]
    for i in range(OWN):
        for j in range(OJW):
            keep = label_ab == (occ_ref[own_i + i] ^ occ_ref[j])
            denominator = occ_e_ref[own_i + i] + occ_e_ref[j] - energy_ab
            scale_ref[i, j] = jnp.where(keep, 1.0, 0.0) / denominator

    pltpu.make_async_copy(w_ref, w_ref, sem).wait()


def prepare(occ_irrep, vir_irrep, occ_energy, vir_energy, w):
    return pl.pallas_call(
        prepare_kernel,
        out_shape=[
            jax.ShapeDtypeStruct((OCC * CW, WIDE), BF16),
            jax.ShapeDtypeStruct((SLOT, VIR), BF16),
            jax.ShapeDtypeStruct((OWN, OJW, SEC, VIR), F32),
        ],
        in_specs=[SMEM] * 4 + [VMEM] * 2 + [HBM],
        out_specs=[VMEM] * 3,
        scratch_shapes=[pltpu.SemaphoreType.DMA],
        compiler_params=pltpu.CompilerParams(vmem_limit_bytes=24 * MIB),
        cost_estimate=pl.CostEstimate(flops=10**8, bytes_accessed=20 * 10**6, transcendentals=0),
        name="prepare",
    )(
        occ_irrep,
        vir_irrep,
        occ_energy,
        vir_energy,
        vir_irrep.reshape(1, VIR),
        vir_energy.reshape(1, VIR),
        w,
    )


def lane_tiles(got_ref, s):
    got = got_ref[s].astype(F32).reshape(ROWS // 8, 8, 128)
    sub = lax.broadcasted_iota(jnp.int32, (8, 128), 0)
    tiles = []
    for t in range(TILES):
        n, j = divmod(t, 4)
        if j < 3:
            tiles.append(got[3 * n + j])
        else:
            a, b, c = (pltpu.roll(got[3 * n + j], 2 + 2 * j, 0) for j in range(3))
            tiles.append(jnp.where(sub < 2, a, jnp.where(sub < 4, b, c)))
    return tiles


def term_kernel(occ_ref, vir_ref, label_ref, got_ref, fold_ref, w_hbm, *refs):
    outs, own_ref, refs = refs[:3], refs[3], refs[4:]
    a_ref, b_ref, w_ref, sum_ref, masked_ref, sems = refs[:6]
    lhs_refs = refs[6:]
    me = lax.axis_index("con")

    def fetch(step):
        return pltpu.make_async_copy(w_hbm.at[pl.ds(step * BLOCK, BLOCK)], w_ref.at[step], sems.at[step])

    for step in range(STEPS):
        fetch(step).start()

    lane2 = lax.broadcasted_iota(jnp.int32, (8, 128), 1)

    def unpack(h, carry):
        last_a = last_b = None
        for n in range(4):
            tiles = lane_tiles(got_ref, 4 * h + n)
            units_a, units_b = tiles[:COUPLES], tiles[COUPLES:]
            if n % 2:
                units_a[0] = jnp.where(lane2 < 64, last_a, units_a[0])
            if n > 0:
                units_b[0] = jnp.where(lane2 < 32 * n, last_b, units_b[0])
            last_a, last_b = units_a[-1], units_b[-1]
            for u in range(COUPLES if n % 2 else COUPLES - 1):
                a_ref[50 * h + 25 * n // 2 + u] = units_a[u]
            for u in range(7 if n == 3 else 6):
                b_ref[25 * h + 6 * n + u] = units_b[u]
        return carry

    lax.fori_loop(0, GRP // 4, unpack, 0)

    ten = OCC // 4
    lane = lax.broadcasted_iota(jnp.int32, (OCC // 2, 8, 128), 2)
    lane_b = lax.broadcasted_iota(jnp.int32, (ten, 8, 128), 2)
    a_by_i, a_by_m = a_ref.reshape(OCC, OCC // 2, 8, 128), a_ref.reshape(ten, 4, OCC // 2, 8, 128)
    b_by_i, b_by_m = b_ref.reshape(OCC, ten, 8, 128), b_ref.reshape(ten, 4, ten, 8, 128)

    def crossed_a(kk):
        first, second = a_by_i[2 * kk], a_by_i[2 * kk + 1]
        even = jnp.where(lane < 64, first, pltpu.roll(second, 64, 2)).reshape(ten, 2, 8, 128)
        odd = jnp.where(lane < 64, pltpu.roll(first, 64, 2), second).reshape(ten, 2, 8, 128)
        return even[:, 0], odd[:, 0], even[:, 1], odd[:, 1]

    def crossed_b(kq):
        c = [b_by_i[4 * kq + n] for n in range(4)]
        low, upper = lane_b < 64, lane_b % 64 >= 32
        wide = []
        for n in range(2):
            wide.append(jnp.where(low, c[n], pltpu.roll(c[n + 2], 64, 2)))
        for n in range(2):
            wide.append(jnp.where(low, pltpu.roll(c[n], 64, 2), c[n + 2]))
        found = []
        for m in (0, 2):
            found.append(jnp.where(upper, pltpu.roll(wide[m + 1], 32, 2), wide[m]))
            found.append(jnp.where(upper, wide[m + 1], pltpu.roll(wide[m], 96, 2)))
        return found

    def combine(step, n, lanes):
        if step < 2:
            by_m, k, crossed = a_by_m, step * 10 + n, crossed_a(step * 10 + n)
        else:
            by_m, k, crossed = b_by_m, n, crossed_b(n)
        for m in range(4):
            value = 2.0 * by_m[:, m, k] - crossed[m]
            lhs_refs[step][m * ten * 8 : (m + 1) * ten * 8, lanes] = value.reshape(ten * 8, 128).astype(BF16)

    def combine_first(n, carry):
        combine(0, n, pl.ds(pl.multiple_of(n * 128, 128), 128))
        return carry

    lax.fori_loop(0, 10, combine_first, 0)
    for step in range(STEPS):
        fetch(step).wait()
        if step + 1 < STEPS:
            for n in range(10):
                combine(step + 1, n, slice(n * 128, n * 128 + 128))
        part = jnp.dot(lhs_refs[step][...], w_ref[step], preferred_element_type=F32)
        sum_ref[...] = part if step == 0 else sum_ref[...] + part

    label_ab = own_column(vir_ref, lax.axis_index("grp") * SEC, jnp.int32) ^ label_ref[...]
    row = lax.broadcasted_iota(jnp.int32, (64, OWN * 8), 0)
    col = lax.broadcasted_iota(jnp.int32, (64, OWN * 8), 1)
    dense = jnp.where((row < OWN * SEC) & (col == row // SEC * 8 + row % SEC), 1.0, 0.0).astype(BF16)
    for s in range(CON):
        owner = lax.rem(me + s, CON)
        for n in range(OWN):
            i = owner * OWN + n
            rows = pl.ds(pl.multiple_of((lax.rem(i, 4) * ten + lax.div(i, 4)) * 8, 8), 8)
            if s == 0:
                own_ref[n * 8 : n * 8 + 8, :] = sum_ref[rows, :]
                continue
            for j in range(OJW):
                keep = label_ab == (occ_ref[i] ^ occ_ref[j])
                at = (j * OWN + n) * 8
                masked_ref[at : at + 8, :] = jnp.where(keep, sum_ref[rows, j * VIR : (j + 1) * VIR], 0.0)
        if s > 0:
            folded = nt_dot(masked_ref[...].astype(BF16), fold_ref[...]).astype(BF16)
            ends = []
            for j in range(OJW):
                chunk = jnp.dot(dense, folded[j * OWN * 8 : (j + 1) * OWN * 8], preferred_element_type=F32)
                outs[s - 1][64 * j : 64 * j + 64, :] = chunk[:, :128].astype(BF16)
                ends.append(chunk[:, 128:])
            outs[s - 1][192:256, :] = jnp.concatenate(ends[:2], 1).astype(BF16)
            outs[s - 1][256:, :] = jnp.concatenate([ends[2][:32], ends[2][32:]], 1).astype(BF16)


def term(occ_irrep, vir_irrep, got, fold, w):
    return pl.pallas_call(
        term_kernel,
        out_shape=[jax.ShapeDtypeStruct((CHUNK, 128), BF16)] * 3
        + [jax.ShapeDtypeStruct((OWN * 8, WIDE), F32)],
        in_specs=[SMEM, SMEM] + [VMEM] * 3 + [HBM],
        out_specs=[VMEM] * 4,
        scratch_shapes=[
            pltpu.VMEM((OCC * OCC // 2, 8, 128), F32),
            pltpu.VMEM((OCC * OCC // 4, 8, 128), F32),
            pltpu.VMEM((STEPS, BLOCK, WIDE), BF16),
            pltpu.VMEM((OCC * 8, WIDE), F32),
            pltpu.VMEM((OJW * OWN * 8, VIR), F32),
            pltpu.SemaphoreType.DMA((STEPS,)),
        ]
        + [pltpu.VMEM((OCC * 8, BLOCK), BF16)] * STEPS,
        compiler_params=pltpu.CompilerParams(vmem_limit_bytes=TERM_LIMIT),
        name="term",
    )(occ_irrep, vir_irrep, vir_irrep.reshape(1, VIR), got, fold, w)


def unpacked(chunk, j):
    if j < 2:
        end = chunk[192:256, 64 * j : 64 * j + 64]
    else:
        end = jnp.concatenate([chunk[256:, :64], chunk[256:, 64:]], 0)
    return jnp.concatenate([chunk[64 * j : 64 * j + 64, :], end], 1)


def finish_kernel(fold_ref, scale_ref, own_ref, *refs):
    chunks, out_ref = refs[:3], refs[3]
    for j in range(OJW):
        stacked = jnp.concatenate([unpacked(chunk, j) for chunk in chunks], 0)
        parts = jnp.dot(stacked, fold_ref[...], preferred_element_type=F32)
        total = parts[:64] + parts[64:128] + parts[128:]
        for i in range(OWN):
            own = own_ref[i * 8 : i * 8 + SEC, j * VIR : (j + 1) * VIR]
            out_ref[i, j] = (own + total[i * SEC : (i + 1) * SEC]) * scale_ref[i, j]


def finish(fold, scale, own, chunks):
    return pl.pallas_call(
        finish_kernel,
        out_shape=jax.ShapeDtypeStruct((OWN, OJW, SEC, VIR), F32),
        in_specs=[VMEM] * 6,
        out_specs=VMEM,
        compiler_params=pltpu.CompilerParams(vmem_limit_bytes=8 * MIB),
        name="finish",
    )(fold, scale, own, *chunks)


def shards(amplitudes, integrals, occ_energy, vir_energy, occ_irrep, vir_irrep):
    sent = pack(jnp.swapaxes(amplitudes, 1, 2))
    got = lax.all_to_all(sent, "grp", split_axis=0, concat_axis=0, tiled=True)
    w, fold, scale = prepare(
        occ_irrep, vir_irrep, occ_energy, vir_energy, jnp.swapaxes(integrals, 1, 2)
    )
    *chunks, own = term(occ_irrep, vir_irrep, got, fold, w)
    arrived = [lax.ppermute(chunks[s - 1], "con", [(n, (n + s) % CON) for n in range(CON)]) for s in (1, 3, 2)]
    return finish(fold, scale, own, arrived)


def solution(mesh):
    return jax.shard_map(
        shards,
        mesh=mesh,
        in_specs=(P("grp", None, "con"), P(None, "con", None, None), P(), P(), P(), P()),
        out_specs=P("con", None, "grp", None),
        check_vma=False,
    )
```

```python
import jax
import jax.numpy as jnp
from jax import lax
from jax.experimental import pallas as pl
from jax.experimental.pallas import tpu as pltpu
from jax.sharding import PartitionSpec as P


OCC = 40
VIR = 384
OJW = 3
GRP = 64
CON = 4
PAIR = OCC * OCC // GRP
SEC = VIR // GRP
CW = VIR // CON
OWN = OCC // CON
SLOT = VIR // 2
WIDE = OJW * VIR
VMEM = pl.BlockSpec(memory_space=pltpu.VMEM)
SMEM = pl.BlockSpec(memory_space=pltpu.SMEM)
HBM = pl.BlockSpec(memory_space=pltpu.HBM)
MIB = 1024 * 1024
TERM_LIMIT = 50 * MIB
BF16, F32 = jnp.bfloat16, jnp.float32

COUPLES = 13
TILES = 20
ROWS = 120
CHUNK = 288
A_WIDTH, B_WIDTH = 64, 32
STEP_UNITS = (8, 8, 8, 6)
A_UNITS = 20
IN_FLIGHT = 3
LINES = OCC * SEC


def nt_dot(x, y):
    return lax.dot_general(x, y, (((1,), (1,)), ((), ())), preferred_element_type=F32)


def pack_kernel(x_hbm, out_hbm, x_ref, tile_ref, pick_ref, out_ref, sem, out_sem):
    me = lax.axis_index("grp")
    odd, phase = lax.rem(me, 2), lax.rem(me, 4)
    arrivals = []
    for step, (first, last, first_c, last_c) in enumerate(PIECES):
        part = (pl.ds(first, last - first), pl.ds(first_c, last_c - first_c))
        arrivals.append(pltpu.make_async_copy(x_hbm.at[part], x_ref.at[part], sem.at[step]))
        arrivals[-1].start(priority=min(step, 1))
    row = lax.broadcasted_iota(jnp.int32, (GRP * 4, 1), 0)
    dest, sub = row // 8, row % 8
    col = lax.broadcasted_iota(jnp.int32, (GRP * 4, 256), 1)

    def pick(target):
        return jnp.where(col == target, 1.0, 0.0).astype(BF16)

    for half in range(2):
        first = dest * SEC + 64 * half
        main = pick(jnp.where(sub < 6, first + sub, -1))
        for j in range(3):
            pick_ref[half, j, :, :256] = main
            pick_ref[half, j, :, 256:] = pick(jnp.where(sub >= 6, first + 2 * j + sub - 6, -1))

    def place(t, at):
        for p in range(2 if t < COUPLES else 4):
            if t < COUPLES:
                pair, first_c, width = 2 * t + p - odd, 0, A_WIDTH
            else:
                pair, first_c, width = 4 * (t - COUPLES) + p - phase, A_WIDTH, B_WIDTH
            source = x_ref[jnp.clip(pair, 0, PAIR - 1), first_c : first_c + width, :]
            tile_ref[at + p * width : at + (p + 1) * width, :] = source

    sends = []
    for step, groups in enumerate(PACK_STEPS):
        for piece in ARRIVE[step]:
            arrivals[piece].wait()
        size = 128 * len(groups)
        for n, group in enumerate(groups):
            for j in range(4):
                place(4 * group + j, (4 * step + j) * 256 + n * 128)
        for j in range(3):
            main, rest = (slice((4 * step + m) * 256, (4 * step + m) * 256 + size) for m in (j, 3))
            for half in range(2):
                lanes = slice(128 * half, 128 * half + 256)
                both = jnp.concatenate([tile_ref[main, lanes], tile_ref[rest, lanes]], 1)
                value = nt_dot(pick_ref[half, j], both).astype(BF16)
                for n, group in enumerate(groups):
                    tile = value[:, n * 128 : n * 128 + 128].reshape(GRP // 2, 8, 128)
                    at = (3 * group + j) * 8
                    out_ref[half * 32 : half * 32 + 32, at : at + 8, :] = tile
        rows = pl.ds(24 * groups[0], 24 * len(groups))
        sends.append(pltpu.make_async_copy(out_ref.at[:, rows], out_hbm.at[:, rows], out_sem.at[step]))
        sends[-1].start()
    for send in sends:
        send.wait()


PACK_STEPS = ((0, 1), (2, 3), (4,))
PIECES = ((0, 16, 0, A_WIDTH), (16, PAIR, 0, A_WIDTH), (0, PAIR, A_WIDTH, CW))
ARRIVE = ((0,), (1, 2), ())


def pack(x):
    return pl.pallas_call(
        pack_kernel,
        out_shape=jax.ShapeDtypeStruct((GRP, ROWS, 128), BF16),
        in_specs=[HBM],
        out_specs=HBM,
        scratch_shapes=[
            pltpu.VMEM((PAIR, CW, VIR), BF16),
            pltpu.VMEM((len(PACK_STEPS) * 4 * 256, VIR), BF16),
            pltpu.VMEM((2, 3, GRP * 4, 512), BF16),
            pltpu.VMEM((GRP, ROWS, 128), BF16),
            pltpu.SemaphoreType.DMA((len(PIECES),)),
            pltpu.SemaphoreType.DMA((len(PACK_STEPS),)),
        ],
        compiler_params=pltpu.CompilerParams(vmem_limit_bytes=62 * MIB),
        name="pack",
    )(x)


def own_column(ref, first, dtype):
    row = lax.broadcasted_iota(jnp.int32, (8, 1), 0)
    column = jnp.zeros((8, 1), dtype)
    for a in range(SEC):
        column = jnp.where(row == a, ref[first + a], column)
    return column


def prepare_kernel(
    occ_ref, vir_ref, occ_e_ref, vir_e_ref, label_ref, energy_ref, w_hbm, w_ref, fold_ref, scale_ref, line_ref, sem
):
    def fetch(kq, carry):
        for n in range(4):
            for j in range(OJW):
                source = w_hbm.at[4 * kq + n, j]
                lanes = pl.ds(j * VIR, VIR)
                at_a = pl.multiple_of(kq * 256 + n * A_WIDTH, A_WIDTH)
                at_b = pl.multiple_of(OCC * A_WIDTH + kq * 128 + n * B_WIDTH, B_WIDTH)
                pltpu.make_async_copy(
                    source.at[pl.ds(0, A_WIDTH)], w_ref.at[pl.ds(at_a, A_WIDTH), lanes], sem
                ).start()
                pltpu.make_async_copy(
                    source.at[pl.ds(A_WIDTH, B_WIDTH)], w_ref.at[pl.ds(at_b, B_WIDTH), lanes], sem
                ).start()
        return carry

    lax.fori_loop(0, 10, fetch, 0)

    labels = label_ref[...]
    label_row = labels.astype(F32)
    label_col = jnp.transpose(jnp.broadcast_to(label_row, (8, VIR)))[:, :1]
    first = lax.broadcasted_iota(jnp.int32, (VIR, VIR), 0)
    second = lax.broadcasted_iota(jnp.int32, (VIR, VIR), 1)
    ahead = (label_col < label_row) | ((label_col == label_row) & (first < second))
    rank = jnp.sum(jnp.where(ahead, 1.0, 0.0), axis=0, keepdims=True)
    slot = jnp.where(rank >= SLOT, rank - SLOT, rank).astype(jnp.int32)
    fold_ref[...] = jnp.where(lax.broadcasted_iota(jnp.int32, (SLOT, VIR), 0) == slot, 1.0, 0.0).astype(BF16)

    own_i, own_a = lax.axis_index("con") * OWN, lax.axis_index("grp") * SEC
    label_a = own_column(vir_ref, own_a, jnp.int32)[:SEC]
    for i in range(OCC):
        line_ref[i * SEC : (i + 1) * SEC, :] = jnp.broadcast_to(label_a ^ occ_ref[i], (SEC, 128))
    label_ab = label_a ^ labels
    energy_ab = (own_column(vir_e_ref, own_a, F32) + energy_ref[...])[:SEC]
    for i in range(OWN):
        for j in range(OJW):
            keep = label_ab == (occ_ref[own_i + i] ^ occ_ref[j])
            denominator = occ_e_ref[own_i + i] + occ_e_ref[j] - energy_ab
            scale_ref[i, j] = jnp.where(keep, 1.0, 0.0) / denominator

    pltpu.make_async_copy(w_ref, w_ref, sem).wait()


def prepare(occ_irrep, vir_irrep, occ_energy, vir_energy, w):
    return pl.pallas_call(
        prepare_kernel,
        out_shape=[
            jax.ShapeDtypeStruct((OCC * CW, WIDE), BF16),
            jax.ShapeDtypeStruct((SLOT, VIR), BF16),
            jax.ShapeDtypeStruct((OWN, OJW, SEC, VIR), F32),
            jax.ShapeDtypeStruct((LINES, 128), jnp.int32),
        ],
        in_specs=[SMEM] * 4 + [VMEM] * 2 + [HBM],
        out_specs=[VMEM] * 4,
        scratch_shapes=[pltpu.SemaphoreType.DMA],
        compiler_params=pltpu.CompilerParams(vmem_limit_bytes=24 * MIB),
        cost_estimate=pl.CostEstimate(flops=10**8, bytes_accessed=20 * 10**6, transcendentals=0),
        name="prepare",
    )(
        occ_irrep,
        vir_irrep,
        occ_energy,
        vir_energy,
        vir_irrep.reshape(1, VIR),
        vir_energy.reshape(1, VIR),
        w,
    )


def lane_tiles(got_ref, s):
    got = got_ref[s].astype(F32).reshape(ROWS // 8, 8, 128)
    sub = lax.broadcasted_iota(jnp.int32, (8, 128), 0)
    tiles = []
    for t in range(TILES):
        n, j = divmod(t, 4)
        if j < 3:
            tiles.append(got[3 * n + j])
        else:
            a, b, c = (pltpu.roll(got[3 * n + j], 2 + 2 * j, 0) for j in range(3))
            tiles.append(jnp.where(sub < 2, a, jnp.where(sub < 4, b, c)))
    return tiles


def window(ref, first):
    rows = ref[pl.ds(pl.multiple_of(lax.div(first, 8) * 8, 8), 72), :]
    return jnp.where(lax.rem(first, 8) == 0, rows[:64], rows[4:68])


def term_kernel(occ_ref, label_ref, line_ref, got_ref, fold_ref, w_hbm, *refs):
    outs, own_ref, refs = refs[:3], refs[3], refs[4:]
    a_ref, b_ref, w_ref, sum_ref, masked_ref, folded_ref, sems = refs[:7]
    lhs_refs = refs[7:]
    me = lax.axis_index("con")

    def fetch(step):
        rows = pl.ds(128 * sum(STEP_UNITS[:step]), 128 * STEP_UNITS[step])
        return pltpu.make_async_copy(w_hbm.at[rows], w_ref.at[rows], sems.at[step])

    for step in range(IN_FLIGHT):
        fetch(step).start()

    lane2 = lax.broadcasted_iota(jnp.int32, (8, 128), 1)

    def unpack(h, carry):
        last_a = last_b = None
        for n in range(4):
            tiles = lane_tiles(got_ref, 4 * h + n)
            units_a, units_b = tiles[:COUPLES], tiles[COUPLES:]
            if n % 2:
                units_a[0] = jnp.where(lane2 < 64, last_a, units_a[0])
            if n > 0:
                units_b[0] = jnp.where(lane2 < 32 * n, last_b, units_b[0])
            last_a, last_b = units_a[-1], units_b[-1]
            for u in range(COUPLES if n % 2 else COUPLES - 1):
                a_ref[50 * h + 25 * n // 2 + u] = units_a[u]
            for u in range(7 if n == 3 else 6):
                b_ref[25 * h + 6 * n + u] = units_b[u]
        return carry

    lax.fori_loop(0, GRP // 4, unpack, 0)

    ten = OCC // 4
    lane = lax.broadcasted_iota(jnp.int32, (OCC // 2, 8, 128), 2)
    lane_b = lax.broadcasted_iota(jnp.int32, (ten, 8, 128), 2)
    a_by_i, a_by_m = a_ref.reshape(OCC, OCC // 2, 8, 128), a_ref.reshape(ten, 4, OCC // 2, 8, 128)
    b_by_i, b_by_m = b_ref.reshape(OCC, ten, 8, 128), b_ref.reshape(ten, 4, ten, 8, 128)

    def crossed_a(kk):
        first, second = a_by_i[2 * kk], a_by_i[2 * kk + 1]
        even = jnp.where(lane < 64, first, pltpu.roll(second, 64, 2)).reshape(ten, 2, 8, 128)
        odd = jnp.where(lane < 64, pltpu.roll(first, 64, 2), second).reshape(ten, 2, 8, 128)
        return even[:, 0], odd[:, 0], even[:, 1], odd[:, 1]

    def crossed_b(kq):
        c = [b_by_i[4 * kq + n] for n in range(4)]
        low, upper = lane_b < 64, lane_b % 64 >= 32
        wide = []
        for n in range(2):
            wide.append(jnp.where(low, c[n], pltpu.roll(c[n + 2], 64, 2)))
        for n in range(2):
            wide.append(jnp.where(low, pltpu.roll(c[n], 64, 2), c[n + 2]))
        found = []
        for m in (0, 2):
            found.append(jnp.where(upper, pltpu.roll(wide[m + 1], 32, 2), wide[m]))
            found.append(jnp.where(upper, wide[m + 1], pltpu.roll(wide[m], 96, 2)))
        return found

    sub = lax.broadcasted_iota(jnp.int32, (ten, 8, 128), 1)

    def combine(unit):
        if unit < A_UNITS:
            by_m, k, crossed = a_by_m, unit, crossed_a(unit)
        else:
            by_m, k, crossed = b_by_m, unit - A_UNITS, crossed_b(unit - A_UNITS)
        v0, v1, v2, v3 = (2.0 * by_m[:, m, k] - crossed[m] for m in range(4))
        v1, v2, v3 = pltpu.roll(v1, 6, 1), pltpu.roll(v2, 4, 1), pltpu.roll(v3, 2, 1)
        tiles = [jnp.where(sub < 6, v0, v1), jnp.where(sub < 4, v1, v2), jnp.where(sub < 2, v2, v3)]
        return jnp.stack(tiles, 1).reshape(LINES, 128).astype(BF16)

    def combine_step(step):
        first = sum(STEP_UNITS[:step])
        for n in range(STEP_UNITS[step]):
            lhs_refs[step][:, n * 128 : n * 128 + 128] = combine(first + n)

    combine_step(0)
    for step in range(len(STEP_UNITS)):
        fetch(step).wait()
        if step + IN_FLIGHT < len(STEP_UNITS):
            fetch(step + IN_FLIGHT).start()
        if step + 1 < len(STEP_UNITS):
            combine_step(step + 1)
        first = sum(STEP_UNITS[:step])
        w = w_ref[128 * first : 128 * (first + STEP_UNITS[step]), :]
        part = jnp.dot(lhs_refs[step][...], w, preferred_element_type=F32)
        sum_ref[:LINES, :] = part if step == 0 else sum_ref[:LINES, :] + part

    own_ref[...] = window(sum_ref, me * OWN * SEC)
    for j in range(OJW):
        label = line_ref[...] ^ occ_ref[j]
        for n in range(3):
            keep = label == label_ref[:, n * 128 : n * 128 + 128]
            lanes = slice(j * VIR + n * 128, j * VIR + n * 128 + 128)
            masked_ref[j * LINES : (j + 1) * LINES, n * 128 : n * 128 + 128] = jnp.where(
                keep, sum_ref[:LINES, lanes], 0.0
            ).astype(BF16)
    folded_ref[: OJW * LINES, :] = nt_dot(masked_ref[...], fold_ref[...])
    for s in range(1, CON):
        owner = lax.rem(me + s, CON)
        parts = [window(folded_ref, j * LINES + owner * OWN * SEC) for j in range(OJW)]
        ends = [part[:, 128:] for part in parts]
        for j in range(OJW):
            outs[s - 1][64 * j : 64 * j + 64, :] = parts[j][:, :128].astype(BF16)
        outs[s - 1][192:256, :] = jnp.concatenate(ends[:2], 1).astype(BF16)
        outs[s - 1][256:, :] = jnp.concatenate([ends[2][:32], ends[2][32:]], 1).astype(BF16)


def term(occ_irrep, vir_irrep, line_label, got, fold, w):
    return pl.pallas_call(
        term_kernel,
        out_shape=[jax.ShapeDtypeStruct((CHUNK, 128), BF16)] * 3 + [jax.ShapeDtypeStruct((64, WIDE), F32)],
        in_specs=[SMEM] + [VMEM] * 4 + [HBM],
        out_specs=[VMEM] * 4,
        scratch_shapes=[
            pltpu.VMEM((OCC * OCC // 2, 8, 128), F32),
            pltpu.VMEM((OCC * OCC // 4, 8, 128), F32),
            pltpu.VMEM((OCC * CW, WIDE), BF16),
            pltpu.VMEM((LINES + 8, WIDE), F32),
            pltpu.VMEM((OJW * LINES, VIR), BF16),
            pltpu.VMEM((OJW * LINES + 8, SLOT), F32),
            pltpu.SemaphoreType.DMA((len(STEP_UNITS),)),
        ]
        + [pltpu.VMEM((LINES, 128 * units), BF16) for units in STEP_UNITS],
        compiler_params=pltpu.CompilerParams(vmem_limit_bytes=TERM_LIMIT),
        name="term",
    )(occ_irrep, vir_irrep.reshape(1, VIR), line_label, got, fold, w)


def unpacked(chunk, j):
    if j < 2:
        end = chunk[192:256, 64 * j : 64 * j + 64]
    else:
        end = jnp.concatenate([chunk[256:, :64], chunk[256:, 64:]], 0)
    return jnp.concatenate([chunk[64 * j : 64 * j + 64, :], end], 1)


def finish_kernel(fold_ref, scale_ref, own_ref, *refs):
    chunks, out_ref = refs[:3], refs[3]
    for j in range(OJW):
        stacked = jnp.concatenate([unpacked(chunk, j) for chunk in chunks], 0)
        parts = jnp.dot(stacked, fold_ref[...], preferred_element_type=F32)
        total = own_ref[:, j * VIR : (j + 1) * VIR] + (parts[:64] + parts[64:128] + parts[128:])
        for i in range(OWN):
            out_ref[i, j] = total[i * SEC : (i + 1) * SEC] * scale_ref[i, j]


def finish(fold, scale, own, chunks):
    return pl.pallas_call(
        finish_kernel,
        out_shape=jax.ShapeDtypeStruct((OWN, OJW, SEC, VIR), F32),
        in_specs=[VMEM] * 6,
        out_specs=VMEM,
        compiler_params=pltpu.CompilerParams(vmem_limit_bytes=8 * MIB),
        name="finish",
    )(fold, scale, own, *chunks)


def shards(amplitudes, integrals, occ_energy, vir_energy, occ_irrep, vir_irrep):
    sent = pack(jnp.swapaxes(amplitudes, 1, 2))
    got = lax.all_to_all(sent, "grp", split_axis=0, concat_axis=0, tiled=True)
    w, fold, scale, line_label = prepare(
        occ_irrep, vir_irrep, occ_energy, vir_energy, jnp.swapaxes(integrals, 1, 2)
    )
    *chunks, own = term(occ_irrep, vir_irrep, line_label, got, fold, w)
    arrived = [lax.ppermute(chunks[s - 1], "con", [(n, (n + s) % CON) for n in range(CON)]) for s in (3, 1, 2)]
    return finish(fold, scale, own, arrived)


def solution(mesh):
    return jax.shard_map(
        shards,
        mesh=mesh,
        in_specs=(P("grp", None, "con"), P(None, "con", None, None), P(), P(), P(), P()),
        out_specs=P("con", None, "grp", None),
        check_vma=False,
    )
```
